256 devices in a mesh: group: 8 (over y, core), member: 32 (over z, x).
Axes of the slice: x: 4, y: 4, z: 8, core: 2. Of those that a mesh axis runs over, the one named last changes fastest.
Arguments:
- tokens: bfloat16 [1024, 196, 768], P(('group', 'member')), may hold values from -6 to 6
- w_query: bfloat16 [768, 768], replicated, may hold values from -8 to 8
- w_key: bfloat16 [768, 768], replicated, may hold values from -1 to 1
- w_value: bfloat16 [768, 768], replicated, may hold values from -0.21875 to 0.21875
- w_out: bfloat16 [768, 768], replicated, may hold values from -0.21875 to 0.21875
- partners: int32 [1024, 4], P(('group', 'member')), may hold values from 0 to 1023, as said below
- counts: int32 [1024], P(('group', 'member')), may hold values from 1 to 4
- key_slot: int32 [256], P(('group', 'member')), may hold values from 0 to 3
Outputs:
- refined: bfloat16 [1024, 196, 768], P(('group', 'member'))
The draws below stay inside these ranges and needn't reach their ends.
Inputs may be any that keep to these rules, and one draw needn't show every extreme that they name: `partners`: every entry names a view held by another device of the same group; the entries of all views of one device name views of one other device at most 1 times, and those of some other device exactly 1 times.
All inputs are finite; a program needn't handle non-finite values.
Results may differ from the reference program's by a relative error of at most 0.011.
Values may be sent and summed in bfloat16 or wider, within the bound.
No kernel may reach another device: no remote copies, remote signals or barrier semaphores. Data moves between devices by JAX's collectives and lax.ppermute only.
A program may use at most 128 MiB of HBM per device.

```python
import jax
import jax.numpy as jnp
from jax import lax

D = 768
HEADS = 12
SEQ = 196
DEG = 4
VIEWS_DEV = 4
VIEWS = 1024
N_GROUP = 8
N_MEMBER = 32


def draw_tokens(key, part):
    normal_draw = jax.random.normal(key, (VIEWS, SEQ, D), jnp.float32)
    return jnp.clip(normal_draw, -6.0, 6.0).astype(jnp.bfloat16)


def weight_pair(key):
    pair_key = jax.random.fold_in(key, 101)
    key_matrix = jax.random.normal(jax.random.fold_in(pair_key, 1), (D, D), jnp.float32) / jnp.sqrt(jnp.float32(D))
    query_matrix = jax.random.normal(jax.random.fold_in(pair_key, 2), (D, D), jnp.float32) / jnp.sqrt(jnp.float32(D))
    return (jnp.clip(query_matrix, -8.0, 8.0), jnp.clip(key_matrix, -1.0, 1.0))


def draw_w_query(key, part):
    return weight_pair(key)[0].astype(jnp.bfloat16)


def draw_w_key(key, part):
    return weight_pair(key)[1].astype(jnp.bfloat16)


def draw_partners(key, part):
    devices_all = N_GROUP * N_MEMBER
    entry_count = VIEWS_DEV * DEG
    rotation = jax.random.randint(jax.random.fold_in(key, 11), (devices_all, 1), 0, N_MEMBER - 1)
    slots = jax.random.randint(jax.random.fold_in(key, 12), (devices_all, entry_count), 0, VIEWS_DEV)
    device_ids = jnp.arange(devices_all, dtype=jnp.int32)[:, None]
    entry_ids = jnp.arange(entry_count, dtype=jnp.int32)[None, :]
    group_index = device_ids // N_MEMBER
    member_index = device_ids % N_MEMBER
    peers = (member_index + 1 + (entry_ids + rotation) % (N_MEMBER - 1)) % N_MEMBER
    views = (group_index * N_MEMBER + peers) * VIEWS_DEV + slots
    return views.reshape(VIEWS, DEG).astype(jnp.int32)


def with_ends(values, key, low, top_value):
    dims = values.shape
    place = [jax.random.randint(jax.random.fold_in(key, axis), (), 0, dims[axis]) for axis in range(len(dims))]
    values = values.at[tuple(place)].set(low)
    longest = dims.index(max(dims))
    place[longest] = (place[longest] + 1) % dims[longest]
    return values.at[tuple(place)].set(top_value)


def centred(own_key, extent, width, bound, kind=jnp.bfloat16):
    values = width * jax.random.normal(own_key, extent, jnp.float32)
    return jnp.clip(values, min=-bound, max=bound).astype(kind)


def setup_inputs(seed: int = 0) -> dict:
    seeds = jax.random.split(jax.random.key(seed), 9)
    tokens = draw_tokens(jax.random.fold_in(seeds[8], 71), 0)
    w_query = draw_w_query(jax.random.fold_in(seeds[8], 71), 0)
    w_key = draw_w_key(jax.random.fold_in(seeds[8], 71), 0)
    w_value = centred(seeds[3], (D, D), D ** -0.5, 0.21875)
    w_out = centred(seeds[4], (D, D), D ** -0.5, 0.21875)
    partners = draw_partners(jax.random.fold_in(seeds[8], 71), 0)
    counts = with_ends(jax.random.randint(seeds[6], (VIEWS,), 1, DEG + 1), jax.random.fold_in(seeds[6], 1), 1, DEG).astype(jnp.int32)
    key_slot = with_ends(jax.random.randint(seeds[7], (N_GROUP * N_MEMBER,), 0, VIEWS_DEV), jax.random.fold_in(seeds[7], 1), 0, VIEWS_DEV - 1).astype(jnp.int32)
    return {"tokens": tokens, "w_query": w_query, "w_key": w_key, "w_value": w_value, "w_out": w_out, "partners": partners, "counts": counts, "key_slot": key_slot}


def layer_norm(values_in):
    values_in = values_in.astype(jnp.float32)
    centre = lax.optimization_barrier(jnp.mean(values_in, axis=-1, keepdims=True))
    spread = lax.optimization_barrier(jnp.mean((values_in - centre) ** 2, axis=-1, keepdims=True))
    return (values_in - centre) * lax.rsqrt(spread + 1e-05)

def attend(view_query, key_block, value_block, head_count):
    length, features = view_query.shape
    head_size = features // head_count
    entries = key_block.shape[0]
    query_heads = view_query.astype(jnp.float32).reshape(length, head_count, head_size)
    key_heads = key_block.astype(jnp.float32).reshape(entries, length, head_count, head_size)
    value_heads = value_block.astype(jnp.float32).reshape(entries, length, head_count, head_size)
    scores = jnp.einsum('qhd,ekhd->ehqk', query_heads, key_heads) / jnp.sqrt(jnp.float32(head_size))
    probabilities = jax.nn.softmax(scores, axis=-1).astype(jnp.bfloat16)
    outputs = jnp.einsum('ehqk,ekhd->eqhd', probabilities.astype(jnp.float32), value_heads)
    return outputs.reshape(entries, length, features)

def reference(tokens, w_query, w_key, w_value, w_out, partners, counts, key_slot):
    views, length, features = tokens.shape
    normed = layer_norm(tokens).astype(jnp.bfloat16)
    flat_rows = normed.reshape(views * length, features)
    queries = jnp.dot(flat_rows, w_query, preferred_element_type=jnp.float32).astype(jnp.bfloat16).reshape(views, length, features)
    keys_all = jnp.dot(flat_rows, w_key, preferred_element_type=jnp.float32).astype(jnp.bfloat16).reshape(views, length, features)
    values_all = jnp.dot(flat_rows, w_value, preferred_element_type=jnp.float32).astype(jnp.bfloat16).reshape(views, length, features)

    def one_view(view_id):
        device = view_id // VIEWS_DEV
        group_index = device // N_MEMBER
        member_index = device % N_MEMBER
        keyframe = (view_id % VIEWS_DEV == key_slot[device]).astype(jnp.int32)
        below_dev = (group_index - 1) % N_GROUP * N_MEMBER + member_index
        above_dev = (group_index + 1) % N_GROUP * N_MEMBER + member_index
        below_key = below_dev * VIEWS_DEV + key_slot[below_dev]
        above_key = above_dev * VIEWS_DEV + key_slot[above_dev]
        partner_ids = jnp.concatenate([partners[view_id], jnp.stack([below_key, above_key]).astype(jnp.int32)]).astype(jnp.int32)
        outputs = attend(queries[view_id], keys_all[partner_ids], values_all[partner_ids], HEADS)
        divisor = (counts[view_id] + 2 * keyframe).astype(jnp.float32)
        live_weight = (jnp.arange(DEG, dtype=jnp.int32) < counts[view_id]).astype(jnp.float32)
        key_weight = jnp.full((2,), keyframe, jnp.int32).astype(jnp.float32)
        pair_weights = jnp.concatenate([live_weight, key_weight]) / divisor
        return lax.optimization_barrier(jnp.sum(pair_weights[:, None, None] * outputs, axis=0)).astype(jnp.bfloat16)
    mixed = lax.map(one_view, jnp.arange(views, dtype=jnp.int32))
    projected = jnp.dot(mixed.reshape(views * length, features), w_out, preferred_element_type=jnp.float32)
    refined = tokens.astype(jnp.float32) + projected.reshape(views, length, features)
    return refined.astype(jnp.bfloat16)
```

```python
import functools

import jax
import jax.numpy as jnp
from jax import lax
from jax.experimental import pallas as pl
from jax.experimental.pallas import tpu as pltpu
from jax.sharding import Mesh
from jax.sharding import PartitionSpec as P

HEADS = 12
ROWS, COLS = 8, 4
KEY_CODES = (32, 33)
ANY = pl.BlockSpec(memory_space=pl.ANY)
SMEM = pl.BlockSpec(memory_space=pltpu.SMEM)
VMEM = pl.BlockSpec(memory_space=pltpu.VMEM)
VMEM_LIMIT = 40 << 20


def shifted(block, axis, distance):
    n = lax.axis_size(axis)
    return lax.ppermute(block, axis, [(i, (i + distance) % n) for i in range(n)])


def layer_norm(rows):
    rows = rows.astype(jnp.float32)
    centred = rows - jnp.mean(rows, axis=-1, keepdims=True)
    spread = jnp.mean(centred * centred, axis=-1, keepdims=True)
    return (centred * lax.rsqrt(spread + 1e-05)).astype(jnp.bfloat16)


def query_kernel(tokens_ref, w_ref, out_ref):
    normed = layer_norm(tokens_ref[0])
    scale = 1.0 / (tokens_ref.shape[2] // HEADS) ** 0.5
    q = jnp.dot(normed, w_ref[...], preferred_element_type=jnp.float32)
    out_ref[0] = (q * scale).astype(jnp.bfloat16)


def project_queries(tokens, w_query):
    views, length, features = tokens.shape
    return pl.pallas_call(
        query_kernel,
        grid=(views,),
        in_specs=[
            pl.BlockSpec((1, length, features), lambda i: (i, 0, 0)),
            pl.BlockSpec((features, features), lambda i: (0, 0)),
        ],
        out_specs=pl.BlockSpec((1, length, features), lambda i: (i, 0, 0)),
        out_shape=jax.ShapeDtypeStruct(tokens.shape, jnp.bfloat16),
        compiler_params=pltpu.CompilerParams(vmem_limit_bytes=VMEM_LIMIT),
        cost_estimate=pl.CostEstimate(
            flops=2 * views * length * features * features,
            bytes_accessed=4 * views * length * features,
            transcendentals=0,
        ),
        name="queries",
    )(tokens, w_query)


def pick_kernel(picks, n_in, *refs):
    asked, ins, (*outs, held, sem) = refs[: COLS - 1], refs[COLS - 1 :][:n_in], refs[COLS - 1 + n_in :]
    for step, (k, row, _, _, choices) in enumerate(picks):
        place = asked[k - 1][row]
        for source, low, high in choices:

            @pl.when((place >= low) & (place < high))
            def _(source=source, low=low, step=step, place=place):
                pltpu.make_async_copy(
                    ins[source].at[place - low], held.at[step], sem.at[step]
                ).start()

    copies = []
    for step, (_, _, out, lead, choices) in enumerate(picks):
        pltpu.make_async_copy(ins[choices[0][0]].at[0], held.at[step], sem.at[step]).wait()
        copies.append(
            pltpu.make_async_copy(held.at[step], outs[out].at[lead], sem.at[step])
        )
        copies[-1].start()
    for copy in copies:
        copy.wait()


def pick(picks, asked, sources, lead):
    inner = sources[0].shape[1:]
    size = 2 * inner[0] * inner[1]
    return pl.pallas_call(
        functools.partial(pick_kernel, picks, len(sources)),
        in_specs=[SMEM] * len(asked) + [ANY] * len(sources),
        out_specs=[ANY] * len(asked),
        out_shape=[jax.ShapeDtypeStruct((lead, *inner), jnp.bfloat16)] * len(asked),
        scratch_shapes=[
            pltpu.VMEM((len(picks), *inner), jnp.bfloat16),
            pltpu.SemaphoreType.DMA((len(picks),)),
        ],
        cost_estimate=pl.CostEstimate(
            flops=0, bytes_accessed=2 * size * len(picks), transcendentals=0
        ),
        name="pick",
    )(*asked, *sources)

def attend_kernel(slots, n_in, first, keys, entry_ref, place_ref, view_ref, share_ref, *refs):
    q_ref, wk_ref, wv_ref = refs[:3]
    refs = refs[3:]
    if not first:
        acc_in, refs = refs[0], refs[1:]
    ins, (acc, rows_buf, kv, order, sem) = refs[:n_in], refs[n_in:]
    if first:
        acc[...] = jnp.zeros_like(acc)
    else:
        acc[...] = acc_in[...]
    features = q_ref.shape[2]
    pair = 2 * features // HEADS

    count = jnp.int32(0)
    for k, (code, _, _, low, high) in enumerate(slots):
        place = place_ref[code]
        here = (entry_ref[code] >= 0) & (place >= low) & (place < high)

        @pl.when(here)
        def _(k=k, count=count):
            order[count] = k

        count = count + here.astype(jnp.int32)

    def fetch(i):
        slot = order[i]
        for k, (code, source, lead, low, _) in enumerate(slots):

            @pl.when(slot == k)
            def _(code=code, source=source, lead=lead, low=low):
                at = place_ref[code] - low if lead is None else lead
                pltpu.make_async_copy(
                    ins[source].at[at], rows_buf.at[i % 2], sem.at[i % 2]
                ).start()

    @pl.when(count > 0)
    def _():
        fetch(0)

    def entry(i, carry):
        @pl.when(i + 1 < count)
        def _():
            fetch(i + 1)

        pltpu.make_async_copy(ins[0].at[0], rows_buf.at[i % 2], sem.at[i % 2]).wait()
        slot = order[i]
        code = jnp.int32(0)
        for k, (c, *_) in enumerate(slots):
            code = jnp.where(slot == k, c, code)
        e = entry_ref[code]
        view = view_ref[e]
        share = share_ref[e]
        normed = layer_norm(rows_buf[i % 2])
        kv[:, :features] = jnp.dot(
            normed, wk_ref[...], preferred_element_type=jnp.float32
        ).astype(jnp.bfloat16)
        kv[:, features:] = jnp.dot(
            normed, wv_ref[...], preferred_element_type=jnp.float32
        ).astype(jnp.bfloat16)
        length = kv.shape[0]
        low_half = lax.broadcasted_iota(jnp.int32, (length, pair), 1) < pair // 2
        for j in range(HEADS // 2):
            at = slice(j * pair, (j + 1) * pair)
            q2 = q_ref[view, :, at]
            k2 = kv[:keys, at]
            v2 = kv[:keys, features + j * pair : features + (j + 1) * pair]
            parts = []
            for mine in (low_half, ~low_half):
                scores = lax.dot_general(
                    jnp.where(mine, q2, jnp.zeros_like(q2)),
                    k2,
                    (((1,), (1,)), ((), ())),
                    preferred_element_type=jnp.float32,
                )
                weights = jnp.exp(scores - jnp.max(scores, axis=-1, keepdims=True))
                total = jnp.sum(weights, axis=-1, keepdims=True)
                result = jnp.dot(
                    weights.astype(jnp.bfloat16), v2, preferred_element_type=jnp.float32
                )
                parts.append(result * (share / total))
            acc[view, :, at] += jnp.where(low_half, *parts)
        return carry

    lax.fori_loop(0, count, entry, 0)


def attend(slots, tables, queries, w_key, w_value, keys, total, sources):
    views, length, features = queries.shape
    first = total is None
    held = () if first else (total,)
    n_scalar = len(tables)
    work = max(1, len(slots) // 2)
    return pl.pallas_call(
        functools.partial(attend_kernel, slots, len(sources), first, keys),
        in_specs=[SMEM] * n_scalar + [VMEM] * (3 + len(held)) + [ANY] * len(sources),
        out_specs=VMEM,
        out_shape=jax.ShapeDtypeStruct(queries.shape, jnp.float32),
        input_output_aliases={} if first else {n_scalar + 3: 0},
        scratch_shapes=[
            pltpu.VMEM((2, length, features), jnp.bfloat16),
            pltpu.VMEM((length, 2 * features), jnp.bfloat16),
            pltpu.SMEM((len(slots),), jnp.int32),
            pltpu.SemaphoreType.DMA((2,)),
        ],
        compiler_params=pltpu.CompilerParams(vmem_limit_bytes=VMEM_LIMIT),
        cost_estimate=pl.CostEstimate(
            flops=work * 4 * length * features * (features + length),
            bytes_accessed=12 * views * length * features,
            transcendentals=work * HEADS * length * length,
        ),
        name="attend",
    )(*tables, queries, w_key, w_value, *held, *sources)


def output_kernel(total_ref, tokens_ref, w_ref, out_ref):
    mixed = total_ref[0].astype(jnp.bfloat16)
    projected = jnp.dot(mixed, w_ref[...], preferred_element_type=jnp.float32)
    refined = (tokens_ref[0].astype(jnp.float32) + projected).astype(jnp.bfloat16)
    out_ref[0] = refined[: out_ref.shape[1]]


def project_out(total, tokens, w_out, keys):
    views, length, features = tokens.shape
    block = pl.BlockSpec((1, length, features), lambda i: (i, 0, 0))
    return pl.pallas_call(
        output_kernel,
        grid=(views,),
        in_specs=[block, block, pl.BlockSpec((features, features), lambda i: (0, 0))],
        out_specs=pl.BlockSpec((1, keys, features), lambda i: (i, 0, 0)),
        out_shape=jax.ShapeDtypeStruct((views, keys, features), jnp.bfloat16),
        compiler_params=pltpu.CompilerParams(vmem_limit_bytes=VMEM_LIMIT),
        name="output",
    )(total, tokens, w_out)


def per_device(tokens, w_query, w_key, w_value, w_out, partners, counts, key_slot):
    views, length, features = tokens.shape
    degree = partners.shape[1]
    entries = views * degree
    row, column = lax.axis_index("row"), lax.axis_index("column")

    ids = partners.reshape(-1)
    peers = (ids // views) % (ROWS * COLS)
    codes = (peers // COLS - row) % ROWS * COLS + (peers % COLS - column) % COLS
    numbers = jnp.arange(entries, dtype=jnp.int32)
    live = (numbers % degree)[None, :] < jnp.repeat(counts, degree)[None, :]
    hit = (codes[None, :] == jnp.arange(ROWS * COLS, dtype=jnp.int32)[:, None]) & live
    slot_entry = jnp.max(jnp.where(hit, numbers[None, :], -1), axis=1)
    slot_place = jnp.sum(jnp.where(hit, (ids % views)[None, :], 0), axis=1)
    entry_table = jnp.concatenate([slot_entry, jnp.array([entries, entries + 1], jnp.int32)])
    place_table = jnp.concatenate([slot_place, jnp.zeros((2,), jnp.int32)])
    slot_key = key_slot[0]
    view_table = jnp.concatenate([numbers // degree, jnp.stack([slot_key, slot_key])])
    is_key = (jnp.arange(views, dtype=jnp.int32) == slot_key).astype(jnp.int32)
    divisor = 1.0 / (counts + 2 * is_key).astype(jnp.float32)
    key_share = jnp.sum(jnp.where(is_key == 1, divisor, 0.0))
    share_table = jnp.concatenate([jnp.repeat(divisor, degree), jnp.stack([key_share, key_share])])
    tables = (entry_table, place_table, view_table, share_table)

    tokens = jnp.pad(tokens, ((0, 0), (0, -length % 8), (0, 0)))
    down, up = {}, {}
    down[1], up[1] = shifted(tokens, "row", 1), shifted(tokens, "row", -1)
    wanted = slot_place.reshape(ROWS, COLS)
    asked = [shifted(wanted[:, k], "column", k) for k in range(1, COLS)]
    key_view = lax.dynamic_slice_in_dim(tokens, slot_key, 1, axis=0)
    key_below, key_above = shifted(key_view, "group", 1), shifted(key_view, "group", -1)
    queries = project_queries(tokens, w_query)

    full = (0, views)
    halves = [(0, 0, views // 2), (1, views // 2, views)]
    def across(chosen):
        return [shifted(c, "column", -k) for k, c in zip(range(1, COLS), chosen)]

    picks = [(k, 0, k - 1, 0, [(0, 0, views)]) for k in range(1, COLS)]
    chosen = pick(picks, asked, [tokens], 1)
    (down[1], up[1]), chosen, queries = lax.optimization_barrier(((down[1], up[1]), chosen, queries))
    slots = [(c, i, 0, *full) for i, c in enumerate(KEY_CODES)]
    slots += [(k, 1 + k, 0, *full) for k in range(1, COLS)]
    waiting = slots, [key_below, key_above, *across(chosen)]
    total = None
    for s in (1, 2, 3, 4):
        if s < 3:
            down[s + 1], up[s + 1] = shifted(down[s], "row", 1), shifted(up[s], "row", -1)
        elif s == 3:
            down[4] = shifted(down[3][: views // 2], "row", 1)
            up[4] = shifted(up[3][views // 2 :], "row", -1)
        if s < 4:
            picks = [
                (k, r, k - 1, d, [(d, 0, views)])
                for k in range(1, COLS)
                for d, r in enumerate((ROWS - s, s))
            ]
        else:
            picks = [(k, 4, k - 1, 0, halves) for k in range(1, COLS)]
        chosen = pick(picks, asked, [down[s], up[s]], 2 if s < 4 else 1)
        queries, total, chosen = lax.optimization_barrier((queries, total, chosen))
        total = attend(*waiting[:1], tables, queries, w_key, w_value, length, total, waiting[1])
        arrived = across(chosen)
        if s < 4:
            (down[s + 1], up[s + 1]), total, chosen = lax.optimization_barrier(
                ((down[s + 1], up[s + 1]), total, chosen)
            )
            slots = [((ROWS - s) * COLS, 0, None, *full), (s * COLS, 1, None, *full)]
            slots += [
                (r * COLS + k, 1 + k, d, *full)
                for k in range(1, COLS)
                for d, r in enumerate((ROWS - s, s))
            ]
        else:
            slots = [(4 * COLS, h, None, low, high) for h, low, high in halves]
            slots += [(4 * COLS + k, 1 + k, 0, *full) for k in range(1, COLS)]
        waiting = slots, [down[s], up[s], *arrived]
    total = attend(*waiting[:1], tables, queries, w_key, w_value, length, total, waiting[1])
    return project_out(total, tokens, w_out, length)


def solution(mesh):
    finer = Mesh(mesh.devices.reshape(mesh.shape["group"], ROWS, COLS), ("group", "row", "column"))
    everywhere = ("group", "row", "column")
    placed = (
        P(everywhere, None, None),
        P(),
        P(),
        P(),
        P(),
        P(everywhere, None),
        P(everywhere),
        P(everywhere),
    )
    return jax.shard_map(
        per_device,
        mesh=finer,
        in_specs=placed,
        out_specs=P(everywhere, None, None),
        check_vma=False,
    )
```

```python
import functools

import jax
import jax.numpy as jnp
from jax import lax
from jax.experimental import pallas as pl
from jax.experimental.pallas import tpu as pltpu
from jax.sharding import Mesh
from jax.sharding import PartitionSpec as P

HEADS = 12
ROWS, COLS = 8, 4
KEY_CODES = (32, 33)
ANY = pl.BlockSpec(memory_space=pl.ANY)
SMEM = pl.BlockSpec(memory_space=pltpu.SMEM)
VMEM = pl.BlockSpec(memory_space=pltpu.VMEM)
VMEM_LIMIT = 32 << 20
SMALL = pl.CostEstimate(flops=1000, bytes_accessed=1000, transcendentals=0)
LARGE = pl.CostEstimate(flops=60_000_000_000, bytes_accessed=1000, transcendentals=0)
CHUNKS = ((0, 200),)


def shifted(block, axis, distance):
    n = lax.axis_size(axis)
    return lax.ppermute(block, axis, [(i, (i + distance) % n) for i in range(n)])


def layer_norm(rows):
    rows = rows.astype(jnp.float32)
    centred = rows - jnp.mean(rows, axis=-1, keepdims=True)
    spread = jnp.mean(centred * centred, axis=-1, keepdims=True)
    return (centred * lax.rsqrt(spread + 1e-05)).astype(jnp.bfloat16)


def query_kernel(tokens_ref, w_ref, out_ref):
    normed = layer_norm(tokens_ref[0])
    scale = 1.0 / (tokens_ref.shape[2] // HEADS) ** 0.5
    q = jnp.dot(normed, w_ref[...], preferred_element_type=jnp.float32)
    out_ref[0] = (q * scale).astype(jnp.bfloat16)


def project_queries(tokens, w_query):
    views, length, features = tokens.shape
    return pl.pallas_call(
        query_kernel,
        grid=(views,),
        in_specs=[
            pl.BlockSpec((1, length, features), lambda i: (i, 0, 0)),
            pl.BlockSpec((features, features), lambda i: (0, 0)),
        ],
        out_specs=pl.BlockSpec((1, length, features), lambda i: (i, 0, 0)),
        out_shape=jax.ShapeDtypeStruct(tokens.shape, jnp.bfloat16),
        compiler_params=pltpu.CompilerParams(vmem_limit_bytes=VMEM_LIMIT),
        cost_estimate=pl.CostEstimate(
            flops=2 * views * length * features * features,
            bytes_accessed=4 * views * length * features,
            transcendentals=0,
        ),
        name="queries",
    )(tokens, w_query)


def pick_kernel(picks, n_in, *refs):
    asked, ins, (*outs, held, sem) = refs[0], refs[1:][:n_in], refs[1 + n_in :]
    column = lax.axis_index("column")
    for step, (k, row, _, _, choices) in enumerate(picks):
        place = asked[(column + COLS - k) % COLS * ROWS * COLS + row * COLS + k]
        for source, low, high in choices:

            @pl.when((place >= low) & (place < high))
            def _(source=source, low=low, step=step, place=place):
                pltpu.make_async_copy(
                    ins[source].at[place - low], held.at[step], sem.at[step]
                ).start()

    copies = []
    for step, (_, _, out, lead, choices) in enumerate(picks):
        pltpu.make_async_copy(ins[choices[0][0]].at[0], held.at[step], sem.at[step]).wait()
        copies.append(
            pltpu.make_async_copy(held.at[step], outs[out].at[lead], sem.at[step])
        )
        copies[-1].start()
    for copy in copies:
        copy.wait()


def pick(picks, asked, sources, lead):
    inner = sources[0].shape[1:]
    return pl.pallas_call(
        functools.partial(pick_kernel, picks, len(sources)),
        in_specs=[SMEM] + [ANY] * len(sources),
        out_specs=[ANY] * (COLS - 1),
        out_shape=[jax.ShapeDtypeStruct((lead, *inner), jnp.bfloat16)] * (COLS - 1),
        scratch_shapes=[
            pltpu.VMEM((len(picks), *inner), jnp.bfloat16),
            pltpu.SemaphoreType.DMA((len(picks),)),
        ],
        cost_estimate=SMALL,
        name="pick",
    )(asked, *sources)

def attend_kernel(slots, n_in, first, last, keys, entry_ref, place_ref, view_ref, share_ref, *refs):
    q_in, wk_in, wv_in, *refs = refs
    if not first:
        total_in, *refs = refs
    if last:
        tokens_in, wo_in, *refs = refs
    ins, (out, *refs) = refs[:n_in], refs[n_in:]
    rows_buf, kv, order, sem, load_sem, q_ref, wk_ref, wv_ref, *refs = refs
    copies = [(wk_in, wk_ref), (wv_in, wv_ref), (q_in, q_ref)]
    acc = refs[0] if last else out
    if not first:
        copies.append((total_in, acc))
    if last:
        _, tokens_ref, wo_ref = refs
        copies += [(wo_in, wo_ref), (tokens_in, tokens_ref)]
    copies = [
        pltpu.make_async_copy(here, there, load_sem.at[i]) for i, (here, there) in enumerate(copies)
    ]
    features = q_ref.shape[2]
    pair = 2 * features // HEADS

    count = jnp.int32(0)
    for k, (code, _, _, low, high) in enumerate(slots):
        place = place_ref[code]
        here = (entry_ref[code] >= 0) & (place >= low) & (place < high)

        @pl.when(here)
        def _(k=k, count=count):
            order[count] = k

        count = count + here.astype(jnp.int32)

    def parts_of(pieces, at, i):
        row = 0
        for c, source in enumerate(pieces):
            n = ins[source].shape[1]
            yield pltpu.make_async_copy(
                ins[source].at[at], rows_buf.at[i % 2, pl.ds(row, n)], sem.at[i % 2, c]
            )
            row += n

    def fetch(i):
        slot = order[i]
        for k, (code, pieces, lead, low, _) in enumerate(slots):

            @pl.when(slot == k)
            def _(code=code, pieces=pieces, lead=lead, low=low):
                at = place_ref[code] - low if lead is None else lead
                for copy in parts_of(pieces, at, i):
                    copy.start()

    @pl.when(count > 0)
    def _():
        fetch(0)

    for copy in copies:
        copy.start()
    if first:
        acc[...] = jnp.zeros_like(acc)
    late = copies[-2:] if last else []
    for copy in copies[: len(copies) - len(late)]:
        copy.wait()

    def entry(i, carry):
        @pl.when(i + 1 < count)
        def _():
            fetch(i + 1)

        for copy in parts_of(slots[0][1], 0, i):
            copy.wait()
        slot = order[i]
        code = jnp.int32(0)
        for k, (c, *_) in enumerate(slots):
            code = jnp.where(slot == k, c, code)
        e = entry_ref[code]
        view = view_ref[e]
        share = share_ref[e]
        normed = layer_norm(rows_buf[i % 2])
        kv[:, :features] = jnp.dot(
            normed, wk_ref[...], preferred_element_type=jnp.float32
        ).astype(jnp.bfloat16)
        kv[:, features:] = jnp.dot(
            normed, wv_ref[...], preferred_element_type=jnp.float32
        ).astype(jnp.bfloat16)
        low_half = lax.broadcasted_iota(jnp.int32, (kv.shape[0], pair), 1) < pair // 2
        for j in range(HEADS // 2):
            at = slice(j * pair, (j + 1) * pair)
            q2 = q_ref[view, :, at]
            k2 = kv[:keys, at]
            v2 = kv[:keys, features + j * pair : features + (j + 1) * pair]
            parts = []
            for mine in (low_half, ~low_half):
                scores = lax.dot_general(
                    jnp.where(mine, q2, jnp.zeros_like(q2)),
                    k2,
                    (((1,), (1,)), ((), ())),
                    preferred_element_type=jnp.float32,
                )
                weights = jnp.exp(scores - jnp.max(scores, axis=-1, keepdims=True))
                total = jnp.sum(weights, axis=-1, keepdims=True)
                result = jnp.dot(
                    weights.astype(jnp.bfloat16), v2, preferred_element_type=jnp.float32
                )
                parts.append(result * (share / total))
            acc[view, :, at] += jnp.where(low_half, *parts)
        return carry

    lax.fori_loop(0, count, entry, 0)
    for copy in late:
        copy.wait()
    if last:
        for v in range(acc.shape[0]):
            projected = jnp.dot(
                acc[v].astype(jnp.bfloat16), wo_ref[...], preferred_element_type=jnp.float32
            )
            refined = (tokens_ref[v].astype(jnp.float32) + projected).astype(jnp.bfloat16)
            out[v] = refined[:keys]


def attend(slots, tables, queries, w_key, w_value, keys, total, sources, last=()):
    views, length, features = queries.shape
    held = (() if total is None else (total,)) + last
    bf16, f32 = jnp.bfloat16, jnp.float32
    whole = pltpu.VMEM((views, length, features), f32)
    square = pltpu.VMEM((features, features), bf16)
    chunks = len(slots[0][1])
    if last:
        out_shape = jax.ShapeDtypeStruct((views, keys, features), bf16)
    else:
        out_shape = jax.ShapeDtypeStruct((views, length, features), f32)
    return pl.pallas_call(
        functools.partial(attend_kernel, slots, len(sources), total is None, bool(last), keys),
        in_specs=[SMEM] * len(tables) + [ANY] * (3 + len(held) + len(sources)),
        out_specs=VMEM,
        out_shape=out_shape,
        scratch_shapes=[
            pltpu.VMEM((2, length, features), bf16),
            pltpu.VMEM((length, 2 * features), bf16),
            pltpu.SMEM((len(slots),), jnp.int32),
            pltpu.SemaphoreType.DMA((2, chunks)),
            pltpu.SemaphoreType.DMA((3 + len(held),)),
            pltpu.VMEM(queries.shape, bf16),
            square,
            square,
            *((whole, pltpu.VMEM(queries.shape, bf16), square) if last else ()),
        ],
        compiler_params=pltpu.CompilerParams(vmem_limit_bytes=VMEM_LIMIT),
        cost_estimate=LARGE,
        name="attend",
    )(*tables, queries, w_key, w_value, *held, *sources)


def per_device(tokens, w_query, w_key, w_value, w_out, partners, counts, key_slot):
    views, length, features = tokens.shape
    degree = partners.shape[1]
    entries = views * degree
    row, column = lax.axis_index("row"), lax.axis_index("column")

    ids = partners.reshape(-1)
    peers = (ids // views) % (ROWS * COLS)
    codes = (peers // COLS - row) % ROWS * COLS + (peers % COLS - column) % COLS
    numbers = jnp.arange(entries, dtype=jnp.int32)
    live = (numbers % degree)[None, :] < jnp.repeat(counts, degree)[None, :]
    hit = (codes[None, :] == jnp.arange(ROWS * COLS, dtype=jnp.int32)[:, None]) & live
    slot_entry = jnp.max(jnp.where(hit, numbers[None, :], -1), axis=1)
    slot_place = jnp.sum(jnp.where(hit, (ids % views)[None, :], 0), axis=1)
    entry_table = jnp.concatenate([slot_entry, jnp.array([entries, entries + 1], jnp.int32)])
    place_table = jnp.concatenate([slot_place, jnp.zeros((2,), jnp.int32)])
    slot_key = key_slot[0]
    view_table = jnp.concatenate([numbers // degree, jnp.stack([slot_key, slot_key])])
    is_key = (jnp.arange(views, dtype=jnp.int32) == slot_key).astype(jnp.int32)
    divisor = 1.0 / (counts + 2 * is_key).astype(jnp.float32)
    key_share = jnp.sum(jnp.where(is_key == 1, divisor, 0.0))
    share_table = jnp.concatenate([jnp.repeat(divisor, degree), jnp.stack([key_share, key_share])])
    tables = (entry_table, place_table, view_table, share_table)

    tokens = jnp.pad(tokens, ((0, 0), (0, -length % 8), (0, 0)))
    chunks = range(len(CHUNKS))
    own = [tokens[:, low:high] for low, high in CHUNKS]
    down = [own] + [[None] * len(CHUNKS) for _ in range(4)]
    up = [own] + [[None] * len(CHUNKS) for _ in range(4)]

    def pass_on(s, c):
        below, above = down[s][c], up[s][c]
        if s == 3:
            below, above = below[: views // 2], above[views // 2 :]
        down[s + 1][c], up[s + 1][c] = shifted(below, "row", 1), shifted(above, "row", -1)

    for c in chunks:
        pass_on(0, c)
    asked = lax.all_gather(slot_place, "column", tiled=True)
    key_view = lax.dynamic_slice_in_dim(tokens, slot_key, 1, axis=0)
    key_parts = [key_view[:, low:high] for low, high in CHUNKS]
    below = [shifted(x, "group", 1) for x in key_parts]
    above = [shifted(x, "group", -1) for x in key_parts]
    queries = project_queries(tokens, w_query)
    below, above, asked = lax.optimization_barrier((below, above, asked))
    full = (0, views)
    halves = [(0, 0, views // 2), (1, views // 2, views)]

    def across(chosen):
        return [shifted(x, "column", -k) for k, x in zip(range(1, COLS), chosen)]

    picks = [(k, 0, k - 1, 0, [(0, 0, views)]) for k in range(1, COLS)]
    chosen = [pick(picks, asked, [x], 1) for x in own]
    arrived = [across(x) for x in chosen]
    done = queries, arrived
    waiting = [(c, x, 0, *full) for c, x in zip(KEY_CODES, (below, above))]
    waiting += [(k, [a[k - 1] for a in arrived], 0, *full) for k in range(1, COLS)]

    def run(waiting, total, last=()):
        sources, slots = [], []
        for code, arrays, lead, low, high in waiting:
            places = []
            for x in arrays:
                known = [i for i, y in enumerate(sources) if y is x]
                places.append(known[0] if known else len(sources))
                if not known:
                    sources.append(x)
            slots.append((code, tuple(places), lead, low, high))
        return attend(slots, tables, queries, w_key, w_value, length, total, sources, last)

    total = None
    for s in (1, 2, 3, 4):
        for c in chunks:
            (down[s][c], up[s][c]), done = lax.optimization_barrier(((down[s][c], up[s][c]), done))
            if s < 4:
                pass_on(s, c)
                picks = [
                    (k, r, k - 1, d, [(d, 0, views)])
                    for k in range(1, COLS)
                    for d, r in enumerate((ROWS - s, s))
                ]
            else:
                picks = [(k, 4, k - 1, 0, halves) for k in range(1, COLS)]
            chosen[c] = pick(picks, asked, [down[s][c], up[s][c]], 2 if s < 4 else 1)
            arrived[c] = across(chosen[c])
            done = chosen[c]
        if s < 4:
            waiting += [(h * COLS, x, None, *full) for h, x in ((ROWS - s, down[s]), (s, up[s]))]
        else:
            waiting += [(4 * COLS, (down[4], up[4])[h], None, low, high) for h, low, high in halves]
        queries, total, done = lax.optimization_barrier((queries, total, done))
        total = run(waiting, total)
        done = done, total
        ahead = enumerate((ROWS - s, s) if s < 4 else (4,))
        waiting = [
            (r * COLS + k, [a[k - 1] for a in arrived], d, *full)
            for d, r in ahead
            for k in range(1, COLS)
        ]
    return run(waiting, total, last=(tokens, w_out))


def solution(mesh):
    finer = Mesh(mesh.devices.reshape(mesh.shape["group"], ROWS, COLS), ("group", "row", "column"))
    everywhere = ("group", "row", "column")
    placed = (
        P(everywhere, None, None),
        P(),
        P(),
        P(),
        P(),
        P(everywhere, None),
        P(everywhere),
        P(everywhere),
    )
    return jax.shard_map(
        per_device,
        mesh=finer,
        in_specs=placed,
        out_specs=P(everywhere, None, None),
        check_vma=False,
    )
```

```python
import functools

import jax
import jax.numpy as jnp
from jax import lax
from jax.experimental import pallas as pl
from jax.experimental.pallas import tpu as pltpu
from jax.sharding import Mesh
from jax.sharding import PartitionSpec as P

HEADS = 12
ROWS, COLS = 8, 4
KEY_CODES = (32, 33)
ANY = pl.BlockSpec(memory_space=pl.ANY)
SMEM = pl.BlockSpec(memory_space=pltpu.SMEM)
VMEM = pl.BlockSpec(memory_space=pltpu.VMEM)
VMEM_LIMIT = 8 << 20
SMALL = pl.CostEstimate(flops=1000, bytes_accessed=1000, transcendentals=0)
LARGE = pl.CostEstimate(flops=20_000_000_000, bytes_accessed=1000, transcendentals=0)
CHUNKS = ((0, 200),)


def shifted(block, axis, distance):
    n = lax.axis_size(axis)
    return lax.ppermute(block, axis, [(i, (i + distance) % n) for i in range(n)])


def kept(block):
    return pltpu.with_memory_space_constraint(block, pltpu.VMEM)


def layer_norm(rows):
    rows = rows.astype(jnp.float32)
    centred = rows - jnp.mean(rows, axis=-1, keepdims=True)
    spread = jnp.mean(centred * centred, axis=-1, keepdims=True)
    return (centred * lax.rsqrt(spread + 1e-05)).astype(jnp.bfloat16)


def query_kernel(tokens_ref, w_ref, out_ref):
    normed = layer_norm(tokens_ref[0])
    scale = 1.0 / (tokens_ref.shape[2] // HEADS) ** 0.5
    q = jnp.dot(normed, w_ref[...], preferred_element_type=jnp.float32)
    out_ref[0] = (q * scale).astype(jnp.bfloat16)


def project_queries(tokens, w_query):
    views, length, features = tokens.shape
    return pl.pallas_call(
        query_kernel,
        grid=(views,),
        in_specs=[
            pl.BlockSpec((1, length, features), lambda i: (i, 0, 0)),
            pl.BlockSpec((features, features), lambda i: (0, 0)),
        ],
        out_specs=pl.BlockSpec((1, length, features), lambda i: (i, 0, 0)),
        out_shape=jax.ShapeDtypeStruct(tokens.shape, jnp.bfloat16),
        compiler_params=pltpu.CompilerParams(vmem_limit_bytes=VMEM_LIMIT),
        cost_estimate=pl.CostEstimate(
            flops=2 * views * length * features * features,
            bytes_accessed=4 * views * length * features,
            transcendentals=0,
        ),
        name="queries",
    )(tokens, w_query)


def pick_kernel(picks, n_in, *refs):
    asked, ins, (*outs, held, sem) = refs[0], refs[1:][:n_in], refs[1 + n_in :]
    column = lax.axis_index("column")
    for step, (k, row, _, _, choices) in enumerate(picks):
        place = asked[(column + COLS - k) % COLS * ROWS * COLS + row * COLS + k]
        for source, low, high in choices:

            @pl.when((place >= low) & (place < high))
            def _(source=source, low=low, step=step, place=place):
                pltpu.make_async_copy(
                    ins[source].at[place - low], held.at[step], sem.at[step]
                ).start()

    copies = []
    for step, (_, _, out, lead, choices) in enumerate(picks):
        pltpu.make_async_copy(ins[choices[0][0]].at[0], held.at[step], sem.at[step]).wait()
        copies.append(
            pltpu.make_async_copy(held.at[step], outs[out].at[lead], sem.at[step])
        )
        copies[-1].start()
    for copy in copies:
        copy.wait()


def pick(picks, asked, sources, lead):
    inner = sources[0].shape[1:]
    return pl.pallas_call(
        functools.partial(pick_kernel, picks, len(sources)),
        in_specs=[SMEM] + [ANY] * len(sources),
        out_specs=[ANY] * (COLS - 1),
        out_shape=[jax.ShapeDtypeStruct((lead, *inner), jnp.bfloat16)] * (COLS - 1),
        scratch_shapes=[
            pltpu.VMEM((len(picks), *inner), jnp.bfloat16),
            pltpu.SemaphoreType.DMA((len(picks),)),
        ],
        cost_estimate=pl.CostEstimate(flops=2_000_000_000, bytes_accessed=1000, transcendentals=0),
        name="pick",
    )(asked, *sources)

def attend_kernel(slots, n_in, first, last, keys, entry_ref, place_ref, view_ref, share_ref, *refs):
    q_ref, wk_ref, wv_ref, *refs = refs
    if last:
        tokens_ref, wo_ref, *refs = refs
    if not first:
        refs = refs[1:]
    ins, (acc, *refs) = refs[:n_in], refs[n_in:]
    if last:
        out, *refs = refs
    rows_buf, kv, order, sem = refs
    features = q_ref.shape[2]
    pair = 2 * features // HEADS

    count = jnp.int32(0)
    for k, (code, _, _, low, high) in enumerate(slots):
        place = place_ref[code]
        here = (entry_ref[code] >= 0) & (place >= low) & (place < high)

        @pl.when(here)
        def _(k=k, count=count):
            order[count] = k

        count = count + here.astype(jnp.int32)

    def parts_of(pieces, at, i):
        row = 0
        for c, source in enumerate(pieces):
            n = ins[source].shape[1]
            yield pltpu.make_async_copy(
                ins[source].at[at], rows_buf.at[i % 2, pl.ds(row, n)], sem.at[i % 2, c]
            )
            row += n

    def fetch(i):
        slot = order[i]
        for k, (code, pieces, lead, low, _) in enumerate(slots):

            @pl.when(slot == k)
            def _(code=code, pieces=pieces, lead=lead, low=low):
                at = place_ref[code] - low if lead is None else lead
                for copy in parts_of(pieces, at, i):
                    copy.start()

    @pl.when(count > 0)
    def _():
        fetch(0)

    if first:
        acc[...] = jnp.zeros_like(acc)

    def entry(i, carry):
        @pl.when(i + 1 < count)
        def _():
            fetch(i + 1)

        for copy in parts_of(slots[0][1], 0, i):
            copy.wait()
        slot = order[i]
        code = jnp.int32(0)
        for k, (c, *_) in enumerate(slots):
            code = jnp.where(slot == k, c, code)
        e = entry_ref[code]
        view = view_ref[e]
        share = share_ref[e]
        normed = layer_norm(rows_buf[i % 2])
        kv[:, :features] = jnp.dot(
            normed, wk_ref[...], preferred_element_type=jnp.float32
        ).astype(jnp.bfloat16)
        kv[:, features:] = jnp.dot(
            normed, wv_ref[...], preferred_element_type=jnp.float32
        ).astype(jnp.bfloat16)
        low_half = lax.broadcasted_iota(jnp.int32, (kv.shape[0], pair), 1) < pair // 2
        for j in range(HEADS // 2):
            at = slice(j * pair, (j + 1) * pair)
            q2 = q_ref[view, :, at]
            k2 = kv[:keys, at]
            v2 = kv[:keys, features + j * pair : features + (j + 1) * pair]
            parts = []
            for mine in (low_half, ~low_half):
                scores = lax.dot_general(
                    jnp.where(mine, q2, jnp.zeros_like(q2)),
                    k2,
                    (((1,), (1,)), ((), ())),
                    preferred_element_type=jnp.float32,
                )
                weights = jnp.exp(scores - jnp.max(scores, axis=-1, keepdims=True))
                parts.append(
                    jnp.dot(
                        weights.astype(jnp.bfloat16),
                        jnp.where(mine[:keys], v2, jnp.ones_like(v2)),
                        preferred_element_type=jnp.float32,
                    )
                )
            result = jnp.where(low_half, *parts)
            sums = pltpu.roll(jnp.where(low_half, parts[1], parts[0]), pair // 2, 1)
            acc[view, :, at] += result * (share / sums)
        return carry

    lax.fori_loop(0, count, entry, 0)
    if last:
        for v in range(acc.shape[0]):
            projected = jnp.dot(
                acc[v].astype(jnp.bfloat16), wo_ref[...], preferred_element_type=jnp.float32
            )
            refined = (tokens_ref[v].astype(jnp.float32) + projected).astype(jnp.bfloat16)
            out[v] = refined[:keys]


def attend(slots, tables, queries, w_key, w_value, keys, total, sources, last=()):
    views, length, features = queries.shape
    bf16, f32 = jnp.bfloat16, jnp.float32
    known = [queries, w_key, w_value, *last]
    held = [] if total is None else [total]
    at = len(tables) + len(known)
    outs = [pltpu.VMEM((views, length, features), f32)]
    if last:
        outs.append(jax.ShapeDtypeStruct((views, keys, features), bf16))
    return pl.pallas_call(
        functools.partial(attend_kernel, slots, len(sources), total is None, bool(last), keys),
        in_specs=[SMEM] * len(tables) + [VMEM] * len(known + held) + [ANY] * len(sources),
        out_specs=[VMEM] * len(outs),
        out_shape=outs,
        input_output_aliases={at: 0} if held else {},
        scratch_shapes=[
            pltpu.VMEM((2, length, features), bf16),
            pltpu.VMEM((length, 2 * features), bf16),
            pltpu.SMEM((len(slots),), jnp.int32),
            pltpu.SemaphoreType.DMA((2, len(slots[0][1]))),
        ],
        compiler_params=pltpu.CompilerParams(vmem_limit_bytes=VMEM_LIMIT),
        cost_estimate=LARGE,
        name="attend",
    )(*tables, *known, *held, *sources)


def per_device(tokens, w_query, w_key, w_value, w_out, partners, counts, key_slot):
    views, length, features = tokens.shape
    degree = partners.shape[1]
    entries = views * degree
    row, column = lax.axis_index("row"), lax.axis_index("column")

    ids = partners.reshape(-1)
    peers = (ids // views) % (ROWS * COLS)
    codes = (peers // COLS - row) % ROWS * COLS + (peers % COLS - column) % COLS
    numbers = jnp.arange(entries, dtype=jnp.int32)
    live = (numbers % degree)[None, :] < jnp.repeat(counts, degree)[None, :]
    hit = (codes[None, :] == jnp.arange(ROWS * COLS, dtype=jnp.int32)[:, None]) & live
    slot_entry = jnp.max(jnp.where(hit, numbers[None, :], -1), axis=1)
    slot_place = jnp.sum(jnp.where(hit, (ids % views)[None, :], 0), axis=1)
    entry_table = jnp.concatenate([slot_entry, jnp.array([entries, entries + 1], jnp.int32)])
    place_table = jnp.concatenate([slot_place, jnp.zeros((2,), jnp.int32)])
    slot_key = key_slot[0]
    view_table = jnp.concatenate([numbers // degree, jnp.stack([slot_key, slot_key])])
    is_key = (jnp.arange(views, dtype=jnp.int32) == slot_key).astype(jnp.int32)
    divisor = 1.0 / (counts + 2 * is_key).astype(jnp.float32)
    key_share = jnp.sum(jnp.where(is_key == 1, divisor, 0.0))
    share_table = jnp.concatenate([jnp.repeat(divisor, degree), jnp.stack([key_share, key_share])])
    tables = (entry_table, place_table, view_table, share_table)

    tokens = jnp.pad(tokens, ((0, 0), (0, -length % 8), (0, 0)))
    chunks = range(len(CHUNKS))
    own = [tokens[:, low:high] for low, high in CHUNKS]
    down = [own] + [[None] * len(CHUNKS) for _ in range(4)]
    up = [own] + [[None] * len(CHUNKS) for _ in range(4)]

    def pass_on(s, c):
        below, above = down[s][c], up[s][c]
        if s == 3:
            below, above = below[: views // 2], above[views // 2 :]
        down[s + 1][c], up[s + 1][c] = shifted(below, "row", 1), shifted(above, "row", -1)

    for c in chunks:
        pass_on(0, c)
    asked = lax.all_gather(slot_place, "column", tiled=True)
    key_at, _ = lax.optimization_barrier((slot_key, slot_place))
    key_view = lax.dynamic_slice_in_dim(tokens, key_at, 1, axis=0)
    key_parts = [key_view[:, low:high] for low, high in CHUNKS]
    below = [shifted(x, "group", 1) for x in key_parts]
    above = [shifted(x, "group", -1) for x in key_parts]
    queries = project_queries(tokens, w_query)
    below, above, asked = lax.optimization_barrier((below, above, asked))
    queries, w_key, w_value = kept(queries), kept(w_key), kept(w_value)
    full = (0, views)
    halves = [(0, 0, views // 2), (1, views // 2, views)]

    def across(chosen):
        return [shifted(x, "column", -k) for k, x in zip(range(1, COLS), chosen)]

    picks = [(k, 0, k - 1, 0, [(0, 0, views)]) for k in range(1, COLS)]
    chosen = [pick(picks, asked, [x], 1) for x in own]
    arrived = [across(x) for x in chosen]
    done = queries, chosen[-1]
    waiting = [(c, x, 0, *full) for c, x in zip(KEY_CODES, (below, above))]
    waiting += [(k, [a[k - 1] for a in arrived], 0, *full) for k in range(1, COLS)]

    def run(waiting, total, last=()):
        sources, slots = [], []
        for code, arrays, lead, low, high in waiting:
            places = []
            for x in arrays:
                known = [i for i, y in enumerate(sources) if y is x]
                places.append(known[0] if known else len(sources))
                if not known:
                    sources.append(x)
            slots.append((code, tuple(places), lead, low, high))
        return attend(slots, tables, queries, w_key, w_value, length, total, sources, last)

    total = None
    for s in (1, 2, 3, 4):
        for c in chunks:
            (down[s][c], up[s][c]), done = lax.optimization_barrier(((down[s][c], up[s][c]), done))
            if s < 3:
                pass_on(s, c)
            if s < 4:
                picks = [
                    (k, r, k - 1, d, [(d, 0, views)])
                    for k in range(1, COLS)
                    for d, r in enumerate((ROWS - s, s))
                ]
            else:
                picks = [(k, 4, k - 1, 0, halves) for k in range(1, COLS)]
            chosen[c] = pick(picks, asked, [down[s][c], up[s][c]], 2 if s < 4 else 1)
            arrived[c] = across(chosen[c])
            done = chosen[c]
            if s == 3:
                (down[3][c], up[3][c]), done = lax.optimization_barrier(((down[3][c], up[3][c]), done))
                pass_on(3, c)
        if s < 4:
            waiting += [(h * COLS, x, None, *full) for h, x in ((ROWS - s, down[s]), (s, up[s]))]
        else:
            waiting += [(4 * COLS, (down[4], up[4])[h], None, low, high) for h, low, high in halves]
        queries, total, done = lax.optimization_barrier((queries, total, done))
        (total,) = run(waiting, total)
        done = done, total
        ahead = enumerate((ROWS - s, s) if s < 4 else (4,))
        waiting = [
            (r * COLS + k, [a[k - 1] for a in arrived], d, *full)
            for d, r in ahead
            for k in range(1, COLS)
        ]
    return run(waiting, total, last=(kept(tokens), kept(w_out)))[1]


def solution(mesh):
    finer = Mesh(mesh.devices.reshape(mesh.shape["group"], ROWS, COLS), ("group", "row", "column"))
    everywhere = ("group", "row", "column")
    placed = (
        P(everywhere, None, None),
        P(),
        P(),
        P(),
        P(),
        P(everywhere, None),
        P(everywhere),
        P(everywhere),
    )
    return jax.shard_map(
        per_device,
        mesh=finer,
        in_specs=placed,
        out_specs=P(everywhere, None, None),
        check_vma=False,
    )
```

```python
import functools

import jax
import jax.numpy as jnp
from jax import lax
from jax.experimental import pallas as pl
from jax.experimental.pallas import tpu as pltpu
from jax.sharding import Mesh
from jax.sharding import PartitionSpec as P

HEADS = 12
ROWS, COLS = 8, 4
KEY_CODES = (32, 33)
ANY = pl.BlockSpec(memory_space=pl.ANY)
SMEM = pl.BlockSpec(memory_space=pltpu.SMEM)
VMEM = pl.BlockSpec(memory_space=pltpu.VMEM)
VMEM_LIMIT = 8 << 20
SMALL = pl.CostEstimate(flops=1000, bytes_accessed=1000, transcendentals=0)
LARGE = pl.CostEstimate(flops=20_000_000_000, bytes_accessed=1000, transcendentals=0)
CHUNKS = ((0, 200),)


def shifted(block, axis, distance):
    n = lax.axis_size(axis)
    return lax.ppermute(block, axis, [(i, (i + distance) % n) for i in range(n)])


def kept(block):
    return pltpu.with_memory_space_constraint(block, pltpu.VMEM)


def layer_norm(rows):
    rows = rows.astype(jnp.float32)
    centred = rows - jnp.mean(rows, axis=-1, keepdims=True)
    spread = jnp.mean(centred * centred, axis=-1, keepdims=True)
    return (centred * lax.rsqrt(spread + 1e-05)).astype(jnp.bfloat16)


def query_kernel(tokens_ref, w_ref, out_ref):
    normed = layer_norm(tokens_ref[0])
    scale = 1.0 / (tokens_ref.shape[2] // HEADS) ** 0.5
    q = jnp.dot(normed, w_ref[...], preferred_element_type=jnp.float32)
    q = q * scale
    size = tokens_ref.shape[2] // HEADS
    even = lax.broadcasted_iota(jnp.int32, q.shape, 1) // size % 2 == 0
    both = jnp.concatenate([jnp.where(even, q, 0.0), jnp.where(even, 0.0, q)], axis=0)
    out_ref[0] = both.astype(jnp.bfloat16)


def project_queries(tokens, w_query):
    views, length, features = tokens.shape
    return pl.pallas_call(
        query_kernel,
        grid=(views,),
        in_specs=[
            pl.BlockSpec((1, length, features), lambda i: (i, 0, 0)),
            pl.BlockSpec((features, features), lambda i: (0, 0)),
        ],
        out_specs=pl.BlockSpec((1, 2 * length, features), lambda i: (i, 0, 0)),
        out_shape=jax.ShapeDtypeStruct((views, 2 * length, features), jnp.bfloat16),
        compiler_params=pltpu.CompilerParams(vmem_limit_bytes=VMEM_LIMIT),
        cost_estimate=pl.CostEstimate(
            flops=2 * views * length * features * features,
            bytes_accessed=4 * views * length * features,
            transcendentals=0,
        ),
        name="queries",
    )(tokens, w_query)


def pick_kernel(picks, n_in, *refs):
    asked, ins, (*outs, held, sem) = refs[0], refs[1:][:n_in], refs[1 + n_in :]
    column = lax.axis_index("column")
    for step, (k, row, _, _, choices) in enumerate(picks):
        place = asked[(column + COLS - k) % COLS * ROWS * COLS + row * COLS + k]
        for source, low, high in choices:

            @pl.when((place >= low) & (place < high))
            def _(source=source, low=low, step=step, place=place):
                pltpu.make_async_copy(
                    ins[source].at[place - low], held.at[step], sem.at[step]
                ).start()

    copies = []
    for step, (_, _, out, lead, choices) in enumerate(picks):
        pltpu.make_async_copy(ins[choices[0][0]].at[0], held.at[step], sem.at[step]).wait()
        copies.append(
            pltpu.make_async_copy(held.at[step], outs[out].at[lead], sem.at[step])
        )
        copies[-1].start()
    for copy in copies:
        copy.wait()


def pick(picks, asked, sources, lead):
    inner = sources[0].shape[1:]
    return pl.pallas_call(
        functools.partial(pick_kernel, picks, len(sources)),
        in_specs=[SMEM] + [ANY] * len(sources),
        out_specs=[ANY] * (COLS - 1),
        out_shape=[jax.ShapeDtypeStruct((lead, *inner), jnp.bfloat16)] * (COLS - 1),
        scratch_shapes=[
            pltpu.VMEM((len(picks), *inner), jnp.bfloat16),
            pltpu.SemaphoreType.DMA((len(picks),)),
        ],
        cost_estimate=pl.CostEstimate(flops=2_000_000_000, bytes_accessed=1000, transcendentals=0),
        name="pick",
    )(asked, *sources)

def attend_kernel(slots, n_in, first, last, keys, entry_ref, place_ref, view_ref, share_ref, *refs):
    q_ref, wk_ref, wv_ref, *refs = refs
    if last:
        tokens_ref, wo_ref, *refs = refs
    if not first:
        refs = refs[1:]
    ins, (acc, *refs) = refs[:n_in], refs[n_in:]
    if last:
        out, *refs = refs
    rows_buf, kv, order, sem = refs
    features = q_ref.shape[2]
    pair = 2 * features // HEADS

    count = jnp.int32(0)
    for k, (code, _, _, low, high) in enumerate(slots):
        place = place_ref[code]
        here = (entry_ref[code] >= 0) & (place >= low) & (place < high)

        @pl.when(here)
        def _(k=k, count=count):
            order[count] = k

        count = count + here.astype(jnp.int32)

    def parts_of(pieces, at, i):
        row = 0
        for c, source in enumerate(pieces):
            n = ins[source].shape[1]
            yield pltpu.make_async_copy(
                ins[source].at[at], rows_buf.at[i % 2, pl.ds(row, n)], sem.at[i % 2, c]
            )
            row += n

    def fetch(i):
        slot = order[i]
        for k, (code, pieces, lead, low, _) in enumerate(slots):

            @pl.when(slot == k)
            def _(code=code, pieces=pieces, lead=lead, low=low):
                at = place_ref[code] - low if lead is None else lead
                for copy in parts_of(pieces, at, i):
                    copy.start()

    @pl.when(count > 0)
    def _():
        fetch(0)

    if first:
        acc[...] = jnp.zeros_like(acc)

    def entry(i, carry):
        @pl.when(i + 1 < count)
        def _():
            fetch(i + 1)

        for copy in parts_of(slots[0][1], 0, i):
            copy.wait()
        slot = order[i]
        code = jnp.int32(0)
        for k, (c, *_) in enumerate(slots):
            code = jnp.where(slot == k, c, code)
        e = entry_ref[code]
        view = view_ref[e]
        share = share_ref[e]
        normed = layer_norm(rows_buf[i % 2])
        kv[:, :features] = jnp.dot(
            normed, wk_ref[...], preferred_element_type=jnp.float32
        ).astype(jnp.bfloat16)
        kv[:, features:] = jnp.dot(
            normed, wv_ref[...], preferred_element_type=jnp.float32
        ).astype(jnp.bfloat16)
        low_wide = lax.broadcasted_iota(jnp.int32, (kv.shape[0], 2 * pair), 1) % pair < pair // 2
        for j in range(HEADS // 2):
            at = slice(j * pair, (j + 1) * pair)
            q2 = q_ref[view, :, at]
            k2 = kv[:keys, at]
            v2 = kv[:keys, features + j * pair : features + (j + 1) * pair]
            scores = lax.dot_general(
                q2, k2, (((1,), (1,)), ((), ())), preferred_element_type=jnp.float32
            )
            weights = jnp.exp(scores - jnp.max(scores, axis=-1, keepdims=True))
            both = jnp.dot(
                weights.astype(jnp.bfloat16),
                jnp.concatenate([v2, jnp.ones_like(v2)], axis=1),
                preferred_element_type=jnp.float32,
            )
            length = kv.shape[0]
            mine = jnp.where(low_wide, both[:length], both[length:])
            acc[view, :, at] += mine[:, :pair] * (share / mine[:, pair:])
        return carry

    lax.fori_loop(0, count, entry, 0)
    if last:
        for v in range(acc.shape[0]):
            projected = jnp.dot(
                acc[v].astype(jnp.bfloat16), wo_ref[...], preferred_element_type=jnp.float32
            )
            refined = (tokens_ref[v].astype(jnp.float32) + projected).astype(jnp.bfloat16)
            out[v] = refined[:keys]


def attend(slots, tables, queries, w_key, w_value, keys, total, sources, last=()):
    views, length, features = queries.shape
    length //= 2
    bf16, f32 = jnp.bfloat16, jnp.float32
    known = [queries, w_key, w_value, *last]
    held = [] if total is None else [total]
    at = len(tables) + len(known)
    outs = [pltpu.VMEM((views, length, features), f32)]
    if last:
        outs.append(jax.ShapeDtypeStruct((views, keys, features), bf16))
    return pl.pallas_call(
        functools.partial(attend_kernel, slots, len(sources), total is None, bool(last), keys),
        in_specs=[SMEM] * len(tables) + [VMEM] * len(known + held) + [ANY] * len(sources),
        out_specs=[VMEM] * len(outs),
        out_shape=outs,
        input_output_aliases={at: 0} if held else {},
        scratch_shapes=[
            pltpu.VMEM((2, length, features), bf16),
            pltpu.VMEM((length, 2 * features), bf16),
            pltpu.SMEM((len(slots),), jnp.int32),
            pltpu.SemaphoreType.DMA((2, len(slots[0][1]))),
        ],
        compiler_params=pltpu.CompilerParams(vmem_limit_bytes=VMEM_LIMIT),
        cost_estimate=LARGE,
        name="attend",
    )(*tables, *known, *held, *sources)


def per_device(tokens, w_query, w_key, w_value, w_out, partners, counts, key_slot):
    views, length, features = tokens.shape
    degree = partners.shape[1]
    entries = views * degree
    row, column = lax.axis_index("row"), lax.axis_index("column")

    ids = partners.reshape(-1)
    peers = (ids // views) % (ROWS * COLS)
    codes = (peers // COLS - row) % ROWS * COLS + (peers % COLS - column) % COLS
    numbers = jnp.arange(entries, dtype=jnp.int32)
    live = (numbers % degree)[None, :] < jnp.repeat(counts, degree)[None, :]
    hit = (codes[None, :] == jnp.arange(ROWS * COLS, dtype=jnp.int32)[:, None]) & live
    slot_entry = jnp.max(jnp.where(hit, numbers[None, :], -1), axis=1)
    slot_place = jnp.sum(jnp.where(hit, (ids % views)[None, :], 0), axis=1)
    entry_table = jnp.concatenate([slot_entry, jnp.array([entries, entries + 1], jnp.int32)])
    place_table = jnp.concatenate([slot_place, jnp.zeros((2,), jnp.int32)])
    slot_key = key_slot[0]
    view_table = jnp.concatenate([numbers // degree, jnp.stack([slot_key, slot_key])])
    is_key = (jnp.arange(views, dtype=jnp.int32) == slot_key).astype(jnp.int32)
    divisor = 1.0 / (counts + 2 * is_key).astype(jnp.float32)
    key_share = jnp.sum(jnp.where(is_key == 1, divisor, 0.0))
    share_table = jnp.concatenate([jnp.repeat(divisor, degree), jnp.stack([key_share, key_share])])
    tables = (entry_table, place_table, view_table, share_table)

    tokens = jnp.pad(tokens, ((0, 0), (0, -length % 8), (0, 0)))
    chunks = range(len(CHUNKS))
    own = [tokens[:, low:high] for low, high in CHUNKS]
    down = [own] + [[None] * len(CHUNKS) for _ in range(4)]
    up = [own] + [[None] * len(CHUNKS) for _ in range(4)]

    def pass_on(s, c):
        below, above = down[s][c], up[s][c]
        if s == 3:
            below, above = below[: views // 2], above[views // 2 :]
        down[s + 1][c], up[s + 1][c] = shifted(below, "row", 1), shifted(above, "row", -1)

    for c in chunks:
        pass_on(0, c)
    asked = lax.all_gather(slot_place, "column", tiled=True)
    key_at, _ = lax.optimization_barrier((slot_key, slot_place))
    key_view = lax.dynamic_slice_in_dim(tokens, key_at, 1, axis=0)
    key_parts = [key_view[:, low:high] for low, high in CHUNKS]
    below = [shifted(x, "group", 1) for x in key_parts]
    above = [shifted(x, "group", -1) for x in key_parts]
    queries = project_queries(tokens, w_query)
    below, above, asked = lax.optimization_barrier((below, above, asked))
    queries, w_key, w_value = kept(queries), kept(w_key), kept(w_value)
    full = (0, views)
    halves = [(0, 0, views // 2), (1, views // 2, views)]

    def across(chosen):
        return [shifted(x, "column", -k) for k, x in zip(range(1, COLS), chosen)]

    picks = [(k, 0, k - 1, 0, [(0, 0, views)]) for k in range(1, COLS)]
    chosen = [pick(picks, asked, [x], 1) for x in own]
    arrived = [across(x) for x in chosen]
    done = queries, chosen[-1]
    waiting = [(c, x, 0, *full) for c, x in zip(KEY_CODES, (below, above))]
    waiting += [(k, [a[k - 1] for a in arrived], 0, *full) for k in range(1, COLS)]

    def run(waiting, total, last=()):
        sources, slots = [], []
        for code, arrays, lead, low, high in waiting:
            places = []
            for x in arrays:
                known = [i for i, y in enumerate(sources) if y is x]
                places.append(known[0] if known else len(sources))
                if not known:
                    sources.append(x)
            slots.append((code, tuple(places), lead, low, high))
        return attend(slots, tables, queries, w_key, w_value, length, total, sources, last)

    total = None
    for s in (1, 2, 3, 4):
        for c in chunks:
            (down[s][c], up[s][c]), done = lax.optimization_barrier(((down[s][c], up[s][c]), done))
            if s < 3:
                pass_on(s, c)
            if s < 4:
                picks = [
                    (k, r, k - 1, d, [(d, 0, views)])
                    for k in range(1, COLS)
                    for d, r in enumerate((ROWS - s, s))
                ]
            else:
                picks = [(k, 4, k - 1, 0, halves) for k in range(1, COLS)]
            chosen[c] = pick(picks, asked, [down[s][c], up[s][c]], 2 if s < 4 else 1)
            arrived[c] = across(chosen[c])
            done = chosen[c]
            if s == 3:
                (down[3][c], up[3][c]), done = lax.optimization_barrier(((down[3][c], up[3][c]), done))
                pass_on(3, c)
        if s < 4:
            waiting += [(h * COLS, x, None, *full) for h, x in ((ROWS - s, down[s]), (s, up[s]))]
        else:
            waiting += [(4 * COLS, (down[4], up[4])[h], None, low, high) for h, low, high in halves]
        queries, total, done = lax.optimization_barrier((queries, total, done))
        (total,) = run(waiting, total)
        done = done, total
        ahead = enumerate((ROWS - s, s) if s < 4 else (4,))
        waiting = [
            (r * COLS + k, [a[k - 1] for a in arrived], d, *full)
            for d, r in ahead
            for k in range(1, COLS)
        ]
    return run(waiting, total, last=(kept(tokens), kept(w_out)))[1]


def solution(mesh):
    finer = Mesh(mesh.devices.reshape(mesh.shape["group"], ROWS, COLS), ("group", "row", "column"))
    everywhere = ("group", "row", "column")
    placed = (
        P(everywhere, None, None),
        P(),
        P(),
        P(),
        P(),
        P(everywhere, None),
        P(everywhere),
        P(everywhere),
    )
    return jax.shard_map(
        per_device,
        mesh=finer,
        in_specs=placed,
        out_specs=P(everywhere, None, None),
        check_vma=False,
    )
```

```python
import functools

import jax
import jax.numpy as jnp
from jax import lax
from jax.experimental import pallas as pl
from jax.experimental.pallas import tpu as pltpu
from jax.sharding import Mesh
from jax.sharding import PartitionSpec as P

HEADS = 12
ROWS, COLS = 8, 4
KEY_CODES = (32, 33)
ANY = pl.BlockSpec(memory_space=pl.ANY)
SMEM = pl.BlockSpec(memory_space=pltpu.SMEM)
VMEM = pl.BlockSpec(memory_space=pltpu.VMEM)
HBM = pl.BlockSpec(memory_space=pltpu.HBM)
VMEM_LIMIT = 8 << 20
SMALL = pl.CostEstimate(flops=1000, bytes_accessed=1000, transcendentals=0)
LARGE = pl.CostEstimate(flops=20_000_000_000, bytes_accessed=1000, transcendentals=0)
CHUNKS = ((0, 200),)


def shifted(block, axis, distance):
    n = lax.axis_size(axis)
    return lax.ppermute(block, axis, [(i, (i + distance) % n) for i in range(n)])


def kept(block):
    return pltpu.with_memory_space_constraint(block, pltpu.VMEM)


def in_hbm(block):
    return pltpu.with_memory_space_constraint(block, pltpu.HBM)


def layer_norm(rows):
    rows = rows.astype(jnp.float32)
    centred = rows - jnp.mean(rows, axis=-1, keepdims=True)
    spread = jnp.mean(centred * centred, axis=-1, keepdims=True)
    return (centred * lax.rsqrt(spread + 1e-05)).astype(jnp.bfloat16)


def query_kernel(tokens_ref, w_ref, out_ref):
    normed = layer_norm(tokens_ref[0])
    scale = 1.0 / (tokens_ref.shape[2] // HEADS) ** 0.5
    q = jnp.dot(normed, w_ref[...], preferred_element_type=jnp.float32)
    q = q * scale
    size = tokens_ref.shape[2] // HEADS
    even = lax.broadcasted_iota(jnp.int32, q.shape, 1) // size % 2 == 0
    both = jnp.concatenate([jnp.where(even, q, 0.0), jnp.where(even, 0.0, q)], axis=0)
    out_ref[0] = both.astype(jnp.bfloat16)


def project_queries(tokens, w_query):
    views, length, features = tokens.shape
    return pl.pallas_call(
        query_kernel,
        grid=(views,),
        in_specs=[
            pl.BlockSpec((1, length, features), lambda i: (i, 0, 0)),
            pl.BlockSpec((features, features), lambda i: (0, 0)),
        ],
        out_specs=pl.BlockSpec((1, 2 * length, features), lambda i: (i, 0, 0)),
        out_shape=jax.ShapeDtypeStruct((views, 2 * length, features), jnp.bfloat16),
        compiler_params=pltpu.CompilerParams(vmem_limit_bytes=VMEM_LIMIT),
        cost_estimate=pl.CostEstimate(
            flops=2 * views * length * features * features,
            bytes_accessed=4 * views * length * features,
            transcendentals=0,
        ),
        name="queries",
    )(tokens, w_query)


def pick_kernel(picks, n_in, *refs):
    asked, ins, (*outs, held, sem) = refs[0], refs[1:][:n_in], refs[1 + n_in :]
    column = lax.axis_index("column")
    for step, (k, row, _, _, choices) in enumerate(picks):
        place = asked[(column + COLS - k) % COLS * ROWS * COLS + row * COLS + k]
        for source, low, high in choices:

            @pl.when((place >= low) & (place < high))
            def _(source=source, low=low, step=step, place=place):
                pltpu.make_async_copy(
                    ins[source].at[place - low], held.at[step], sem.at[step]
                ).start()

    copies = []
    for step, (_, _, out, lead, choices) in enumerate(picks):
        pltpu.make_async_copy(ins[choices[0][0]].at[0], held.at[step], sem.at[step]).wait()
        copies.append(
            pltpu.make_async_copy(held.at[step], outs[out].at[lead], sem.at[step])
        )
        copies[-1].start()
    for copy in copies:
        copy.wait()


def pick(picks, asked, sources, lead):
    inner = sources[0].shape[1:]
    return pl.pallas_call(
        functools.partial(pick_kernel, picks, len(sources)),
        in_specs=[SMEM] + [ANY] * len(sources),
        out_specs=[ANY] * (COLS - 1),
        out_shape=[jax.ShapeDtypeStruct((lead, *inner), jnp.bfloat16)] * (COLS - 1),
        scratch_shapes=[
            pltpu.VMEM((len(picks), *inner), jnp.bfloat16),
            pltpu.SemaphoreType.DMA((len(picks),)),
        ],
        cost_estimate=pl.CostEstimate(flops=2_000_000_000, bytes_accessed=1000, transcendentals=0),
        name="pick",
    )(asked, *sources)

def attend_kernel(slots, n_in, first, last, keys, entry_ref, place_ref, view_ref, share_ref, *refs):
    q_ref, wk_ref, wv_ref, *refs = refs
    if last:
        tokens_ref, wo_ref, *refs = refs
    if not first:
        refs = refs[1:]
    ins, (acc, *refs) = refs[:n_in], refs[n_in:]
    if last:
        out, *refs = refs
    rows_buf, kv, order, sem, *refs = refs
    loads = []
    if not last:
        wk_in, wv_in = wk_ref, wv_ref
        wk_ref, wv_ref, load_sem = refs
        loads = [
            pltpu.make_async_copy(wk_in, wk_ref, load_sem.at[0]),
            pltpu.make_async_copy(wv_in, wv_ref, load_sem.at[1]),
        ]
    for load in loads:
        load.start()
    features = q_ref.shape[2]
    pair = 2 * features // HEADS

    count = jnp.int32(0)
    for k, (code, _, _, low, high) in enumerate(slots):
        place = place_ref[code]
        here = (entry_ref[code] >= 0) & (place >= low) & (place < high)

        @pl.when(here)
        def _(k=k, count=count):
            order[count] = k

        count = count + here.astype(jnp.int32)

    def parts_of(pieces, at, i):
        row = 0
        for c, source in enumerate(pieces):
            n = ins[source].shape[1]
            yield pltpu.make_async_copy(
                ins[source].at[at], rows_buf.at[i % 2, pl.ds(row, n)], sem.at[i % 2, c]
            )
            row += n

    def fetch(i):
        slot = order[i]
        for k, (code, pieces, lead, low, _) in enumerate(slots):

            @pl.when(slot == k)
            def _(code=code, pieces=pieces, lead=lead, low=low):
                at = place_ref[code] - low if lead is None else lead
                for copy in parts_of(pieces, at, i):
                    copy.start()

    @pl.when(count > 0)
    def _():
        fetch(0)

    if first:
        acc[...] = jnp.zeros_like(acc)
    for load in loads:
        load.wait()

    def entry(i, carry):
        @pl.when(i + 1 < count)
        def _():
            fetch(i + 1)

        for copy in parts_of(slots[0][1], 0, i):
            copy.wait()
        slot = order[i]
        code = jnp.int32(0)
        for k, (c, *_) in enumerate(slots):
            code = jnp.where(slot == k, c, code)
        e = entry_ref[code]
        view = view_ref[e]
        share = share_ref[e]
        normed = layer_norm(rows_buf[i % 2])
        kv[:, :features] = jnp.dot(
            normed, wk_ref[...], preferred_element_type=jnp.float32
        ).astype(jnp.bfloat16)
        kv[:, features:] = jnp.dot(
            normed, wv_ref[...], preferred_element_type=jnp.float32
        ).astype(jnp.bfloat16)
        low_wide = lax.broadcasted_iota(jnp.int32, (kv.shape[0], 2 * pair), 1) % pair < pair // 2
        for j in range(HEADS // 2):
            at = slice(j * pair, (j + 1) * pair)
            q2 = q_ref[view, :, at]
            k2 = kv[:keys, at]
            v2 = kv[:keys, features + j * pair : features + (j + 1) * pair]
            scores = lax.dot_general(
                q2, k2, (((1,), (1,)), ((), ())), preferred_element_type=jnp.float32
            )
            weights = jnp.exp(scores - jnp.max(scores, axis=-1, keepdims=True))
            both = jnp.dot(
                weights.astype(jnp.bfloat16),
                jnp.concatenate([v2, jnp.ones_like(v2)], axis=1),
                preferred_element_type=jnp.float32,
            )
            length = kv.shape[0]
            mine = jnp.where(low_wide, both[:length], both[length:])
            acc[view, :, at] += mine[:, :pair] * (share / mine[:, pair:])
        return carry

    lax.fori_loop(0, count, entry, 0)
    if last:
        for v in range(acc.shape[0]):
            projected = jnp.dot(
                acc[v].astype(jnp.bfloat16), wo_ref[...], preferred_element_type=jnp.float32
            )
            refined = (tokens_ref[v].astype(jnp.float32) + projected).astype(jnp.bfloat16)
            out[v] = refined[:keys]


def attend(slots, tables, queries, w_key, w_value, keys, total, sources, last=()):
    views, length, features = queries.shape
    length //= 2
    bf16, f32 = jnp.bfloat16, jnp.float32
    weights = [kept(w_key), kept(w_value)] if last else [in_hbm(w_key), in_hbm(w_value)]
    known = [queries, *weights, *last]
    weight_specs = [VMEM if last else HBM] * len(weights)
    square = pltpu.VMEM((features, features), bf16)
    held = [] if total is None else [total]
    at = len(tables) + len(known)
    outs = [pltpu.VMEM((views, length, features), f32)]
    if last:
        outs.append(jax.ShapeDtypeStruct((views, keys, features), bf16))
    return pl.pallas_call(
        functools.partial(attend_kernel, slots, len(sources), total is None, bool(last), keys),
        in_specs=[SMEM] * len(tables)
        + [VMEM, *weight_specs]
        + [VMEM] * (len(last) + len(held))
        + [ANY] * len(sources),
        out_specs=[VMEM] * len(outs),
        out_shape=outs,
        input_output_aliases={at: 0} if held else {},
        scratch_shapes=[
            pltpu.VMEM((2, length, features), bf16),
            pltpu.VMEM((length, 2 * features), bf16),
            pltpu.SMEM((len(slots),), jnp.int32),
            pltpu.SemaphoreType.DMA((2, len(slots[0][1]))),
            *(() if last else (square, square, pltpu.SemaphoreType.DMA((2,)))),
        ],
        compiler_params=pltpu.CompilerParams(vmem_limit_bytes=VMEM_LIMIT),
        cost_estimate=LARGE,
        name="attend",
    )(*tables, *known, *held, *sources)


def per_device(tokens, w_query, w_key, w_value, w_out, partners, counts, key_slot):
    views, length, features = tokens.shape
    degree = partners.shape[1]
    entries = views * degree
    row, column = lax.axis_index("row"), lax.axis_index("column")

    ids = partners.reshape(-1)
    peers = (ids // views) % (ROWS * COLS)
    codes = (peers // COLS - row) % ROWS * COLS + (peers % COLS - column) % COLS
    numbers = jnp.arange(entries, dtype=jnp.int32)
    live = (numbers % degree)[None, :] < jnp.repeat(counts, degree)[None, :]
    hit = (codes[None, :] == jnp.arange(ROWS * COLS, dtype=jnp.int32)[:, None]) & live
    slot_entry = jnp.max(jnp.where(hit, numbers[None, :], -1), axis=1)
    slot_place = jnp.sum(jnp.where(hit, (ids % views)[None, :], 0), axis=1)
    entry_table = jnp.concatenate([slot_entry, jnp.array([entries, entries + 1], jnp.int32)])
    place_table = jnp.concatenate([slot_place, jnp.zeros((2,), jnp.int32)])
    slot_key = key_slot[0]
    view_table = jnp.concatenate([numbers // degree, jnp.stack([slot_key, slot_key])])
    is_key = (jnp.arange(views, dtype=jnp.int32) == slot_key).astype(jnp.int32)
    divisor = 1.0 / (counts + 2 * is_key).astype(jnp.float32)
    key_share = jnp.sum(jnp.where(is_key == 1, divisor, 0.0))
    share_table = jnp.concatenate([jnp.repeat(divisor, degree), jnp.stack([key_share, key_share])])
    tables = (entry_table, place_table, view_table, share_table)

    tokens = jnp.pad(tokens, ((0, 0), (0, -length % 8), (0, 0)))
    chunks = range(len(CHUNKS))
    own = [tokens[:, low:high] for low, high in CHUNKS]
    down = [own] + [[None] * len(CHUNKS) for _ in range(4)]
    up = [own] + [[None] * len(CHUNKS) for _ in range(4)]

    def pass_on(s, c):
        below, above = down[s][c], up[s][c]
        if s == 3:
            below, above = below[: views // 2], above[views // 2 :]
        down[s + 1][c], up[s + 1][c] = shifted(below, "row", 1), shifted(above, "row", -1)

    for c in chunks:
        pass_on(0, c)
    asked = lax.all_gather(slot_place, "column", tiled=True)
    key_at, _ = lax.optimization_barrier((slot_key, slot_place))
    key_view = lax.dynamic_slice_in_dim(tokens, key_at, 1, axis=0)
    key_parts = [key_view[:, low:high] for low, high in CHUNKS]
    below = [shifted(x, "group", 1) for x in key_parts]
    above = [shifted(x, "group", -1) for x in key_parts]
    queries = project_queries(tokens, w_query)
    below, above, asked = lax.optimization_barrier((below, above, asked))
    queries = kept(queries)
    full = (0, views)
    halves = [(0, 0, views // 2), (1, views // 2, views)]

    def across(chosen):
        return [shifted(x, "column", -k) for k, x in zip(range(1, COLS), chosen)]

    picks = [(k, 0, k - 1, 0, [(0, 0, views)]) for k in range(1, COLS)]
    chosen = [pick(picks, asked, [x], 1) for x in own]
    arrived = [across(x) for x in chosen]
    done = queries, chosen[-1]
    waiting = [(c, x, 0, *full) for c, x in zip(KEY_CODES, (below, above))]
    waiting += [(k, [a[k - 1] for a in arrived], 0, *full) for k in range(1, COLS)]

    def run(waiting, total, last=()):
        sources, slots = [], []
        for code, arrays, lead, low, high in waiting:
            places = []
            for x in arrays:
                known = [i for i, y in enumerate(sources) if y is x]
                places.append(known[0] if known else len(sources))
                if not known:
                    sources.append(x)
            slots.append((code, tuple(places), lead, low, high))
        return attend(slots, tables, queries, w_key, w_value, length, total, sources, last)

    total = None
    for s in (1, 2, 3, 4):
        for c in chunks:
            (down[s][c], up[s][c]), done = lax.optimization_barrier(((down[s][c], up[s][c]), done))
            if s < 3:
                pass_on(s, c)
            if s < 4:
                picks = [
                    (k, r, k - 1, d, [(d, 0, views)])
                    for k in range(1, COLS)
                    for d, r in enumerate((ROWS - s, s))
                ]
            else:
                picks = [(k, 4, k - 1, 0, halves) for k in range(1, COLS)]
            chosen[c] = pick(picks, asked, [down[s][c], up[s][c]], 2 if s < 4 else 1)
            arrived[c] = across(chosen[c])
            done = chosen[c]
            if s == 3:
                (down[3][c], up[3][c]), done = lax.optimization_barrier(((down[3][c], up[3][c]), done))
                pass_on(3, c)
        if s < 4:
            waiting += [(h * COLS, x, None, *full) for h, x in ((ROWS - s, down[s]), (s, up[s]))]
        else:
            waiting += [(4 * COLS, (down[4], up[4])[h], None, low, high) for h, low, high in halves]
        queries, total, done = lax.optimization_barrier((queries, total, done))
        (total,) = run(waiting, total)
        done = done, total
        ahead = enumerate((ROWS - s, s) if s < 4 else (4,))
        waiting = [
            (r * COLS + k, [a[k - 1] for a in arrived], d, *full)
            for d, r in ahead
            for k in range(1, COLS)
        ]
    return run(waiting, total, last=(kept(tokens), kept(w_out)))[1]


def solution(mesh):
    finer = Mesh(mesh.devices.reshape(mesh.shape["group"], ROWS, COLS), ("group", "row", "column"))
    everywhere = ("group", "row", "column")
    placed = (
        P(everywhere, None, None),
        P(),
        P(),
        P(),
        P(),
        P(everywhere, None),
        P(everywhere),
        P(everywhere),
    )
    return jax.shard_map(
        per_device,
        mesh=finer,
        in_specs=placed,
        out_specs=P(everywhere, None, None),
        check_vma=False,
    )
```

```python
import functools

import jax
import jax.numpy as jnp
from jax import lax
from jax.experimental import pallas as pl
from jax.experimental.pallas import tpu as pltpu
from jax.sharding import Mesh
from jax.sharding import PartitionSpec as P

HEADS = 12
ROWS, COLS = 8, 4
KEY_CODES = (32, 33)
ANY = pl.BlockSpec(memory_space=pl.ANY)
SMEM = pl.BlockSpec(memory_space=pltpu.SMEM)
VMEM = pl.BlockSpec(memory_space=pltpu.VMEM)
HBM = pl.BlockSpec(memory_space=pltpu.HBM)
VMEM_LIMIT = 8 << 20
SMALL = pl.CostEstimate(flops=1000, bytes_accessed=1000, transcendentals=0)
LARGE = pl.CostEstimate(flops=20_000_000_000, bytes_accessed=1000, transcendentals=0)
CHUNKS = ((0, 200),)


def shifted(block, axis, distance):
    n = lax.axis_size(axis)
    return lax.ppermute(block, axis, [(i, (i + distance) % n) for i in range(n)])


def kept(block):
    return pltpu.with_memory_space_constraint(block, pltpu.VMEM)


def in_hbm(block):
    return pltpu.with_memory_space_constraint(block, pltpu.HBM)


def layer_norm(rows):
    rows = rows.astype(jnp.float32)
    centred = rows - jnp.mean(rows, axis=-1, keepdims=True)
    spread = jnp.mean(centred * centred, axis=-1, keepdims=True)
    return (centred * lax.rsqrt(spread + 1e-05)).astype(jnp.bfloat16)


def query_kernel(tokens_ref, w_ref, out_ref):
    normed = layer_norm(tokens_ref[0])
    scale = 1.0 / (tokens_ref.shape[2] // HEADS) ** 0.5
    q = jnp.dot(normed, w_ref[...], preferred_element_type=jnp.float32)
    q = q * scale
    size = tokens_ref.shape[2] // HEADS
    even = lax.broadcasted_iota(jnp.int32, q.shape, 1) // size % 2 == 0
    both = jnp.concatenate([jnp.where(even, q, 0.0), jnp.where(even, 0.0, q)], axis=0)
    out_ref[0] = both.astype(jnp.bfloat16)


def project_queries(tokens, w_query):
    views, length, features = tokens.shape
    return pl.pallas_call(
        query_kernel,
        grid=(views,),
        in_specs=[
            pl.BlockSpec((1, length, features), lambda i: (i, 0, 0)),
            pl.BlockSpec((features, features), lambda i: (0, 0)),
        ],
        out_specs=pl.BlockSpec((1, 2 * length, features), lambda i: (i, 0, 0)),
        out_shape=jax.ShapeDtypeStruct((views, 2 * length, features), jnp.bfloat16),
        compiler_params=pltpu.CompilerParams(vmem_limit_bytes=VMEM_LIMIT),
        cost_estimate=pl.CostEstimate(
            flops=2 * views * length * features * features,
            bytes_accessed=4 * views * length * features,
            transcendentals=0,
        ),
        name="queries",
    )(tokens, w_query)


def pick_kernel(picks, n_in, *refs):
    asked, ins, (*outs, held, sem) = refs[0], refs[1:][:n_in], refs[1 + n_in :]
    column = lax.axis_index("column")
    for step, (k, row, _, _, choices) in enumerate(picks):
        place = asked[(column + COLS - k) % COLS * ROWS * COLS + row * COLS + k]
        for source, low, high in choices:

            @pl.when((place >= low) & (place < high))
            def _(source=source, low=low, step=step, place=place):
                pltpu.make_async_copy(
                    ins[source].at[place - low], held.at[step], sem.at[step]
                ).start()

    copies = []
    for step, (_, _, out, lead, choices) in enumerate(picks):
        pltpu.make_async_copy(ins[choices[0][0]].at[0], held.at[step], sem.at[step]).wait()
        copies.append(
            pltpu.make_async_copy(held.at[step], outs[out].at[lead], sem.at[step])
        )
        copies[-1].start()
    for copy in copies:
        copy.wait()


def pick(picks, asked, sources, lead):
    inner = sources[0].shape[1:]
    return pl.pallas_call(
        functools.partial(pick_kernel, picks, len(sources)),
        in_specs=[SMEM] + [ANY] * len(sources),
        out_specs=[ANY] * (COLS - 1),
        out_shape=[jax.ShapeDtypeStruct((lead, *inner), jnp.bfloat16)] * (COLS - 1),
        scratch_shapes=[
            pltpu.VMEM((len(picks), *inner), jnp.bfloat16),
            pltpu.SemaphoreType.DMA((len(picks),)),
        ],
        cost_estimate=pl.CostEstimate(flops=2_000_000_000, bytes_accessed=1000, transcendentals=0),
        name="pick",
    )(asked, *sources)

def attend_kernel(slots, n_in, first, last, keys, entry_ref, place_ref, view_ref, share_ref, *refs):
    q_ref, wk_ref, wv_ref, *refs = refs
    if last:
        tokens_ref, wo_ref, *refs = refs
    if not first:
        total_in, *refs = refs
    ins, (acc, *refs) = refs[:n_in], refs[n_in:]
    if last:
        out, *refs = refs
    rows_buf, kv, order, sem, *refs = refs
    loads = []
    if not last:
        wk_in, wv_in = wk_ref, wv_ref
        wk_ref, wv_ref, load_sem = refs
        loads = [
            pltpu.make_async_copy(wk_in, wk_ref, load_sem.at[0]),
            pltpu.make_async_copy(wv_in, wv_ref, load_sem.at[1]),
        ]
        if not first:
            loads.append(pltpu.make_async_copy(total_in, acc, load_sem.at[2]))
    for load in loads:
        load.start()
    features = q_ref.shape[2]
    pair = 2 * features // HEADS

    count = jnp.int32(0)
    for k, (code, _, _, low, high) in enumerate(slots):
        place = place_ref[code]
        here = (entry_ref[code] >= 0) & (place >= low) & (place < high)

        @pl.when(here)
        def _(k=k, count=count):
            order[count] = k

        count = count + here.astype(jnp.int32)

    def parts_of(pieces, at, i):
        row = 0
        for c, source in enumerate(pieces):
            n = ins[source].shape[1]
            yield pltpu.make_async_copy(
                ins[source].at[at], rows_buf.at[i % 2, pl.ds(row, n)], sem.at[i % 2, c]
            )
            row += n

    def fetch(i):
        slot = order[i]
        for k, (code, pieces, lead, low, _) in enumerate(slots):

            @pl.when(slot == k)
            def _(code=code, pieces=pieces, lead=lead, low=low):
                at = place_ref[code] - low if lead is None else lead
                for copy in parts_of(pieces, at, i):
                    copy.start()

    @pl.when(count > 0)
    def _():
        fetch(0)

    if first:
        acc[...] = jnp.zeros_like(acc)
    for load in loads:
        load.wait()

    def entry(i, carry):
        @pl.when(i + 1 < count)
        def _():
            fetch(i + 1)

        for copy in parts_of(slots[0][1], 0, i):
            copy.wait()
        slot = order[i]
        code = jnp.int32(0)
        for k, (c, *_) in enumerate(slots):
            code = jnp.where(slot == k, c, code)
        e = entry_ref[code]
        view = view_ref[e]
        share = share_ref[e]
        normed = layer_norm(rows_buf[i % 2])
        kv[:, :features] = jnp.dot(
            normed, wk_ref[...], preferred_element_type=jnp.float32
        ).astype(jnp.bfloat16)
        kv[:, features:] = jnp.dot(
            normed, wv_ref[...], preferred_element_type=jnp.float32
        ).astype(jnp.bfloat16)
        low_wide = lax.broadcasted_iota(jnp.int32, (kv.shape[0], 2 * pair), 1) % pair < pair // 2
        for j in range(HEADS // 2):
            at = slice(j * pair, (j + 1) * pair)
            q2 = q_ref[view, :, at]
            k2 = kv[:keys, at]
            v2 = kv[:keys, features + j * pair : features + (j + 1) * pair]
            scores = lax.dot_general(
                q2, k2, (((1,), (1,)), ((), ())), preferred_element_type=jnp.float32
            )
            weights = jnp.exp(scores - jnp.max(scores, axis=-1, keepdims=True))
            both = jnp.dot(
                weights.astype(jnp.bfloat16),
                jnp.concatenate([v2, jnp.ones_like(v2)], axis=1),
                preferred_element_type=jnp.float32,
            )
            length = kv.shape[0]
            mine = jnp.where(low_wide, both[:length], both[length:])
            acc[view, :, at] += mine[:, :pair] * (share / mine[:, pair:])
        return carry

    lax.fori_loop(0, count, entry, 0)
    if last:
        for v in range(acc.shape[0]):
            projected = jnp.dot(
                acc[v].astype(jnp.bfloat16), wo_ref[...], preferred_element_type=jnp.float32
            )
            refined = (tokens_ref[v].astype(jnp.float32) + projected).astype(jnp.bfloat16)
            out[v] = refined[:keys]


def attend(slots, tables, queries, w_key, w_value, keys, total, sources, last=()):
    views, length, features = queries.shape
    length //= 2
    bf16, f32 = jnp.bfloat16, jnp.float32
    weights = [kept(w_key), kept(w_value)] if last else [in_hbm(w_key), in_hbm(w_value)]
    known = [queries, *weights, *last]
    weight_specs = [VMEM if last else HBM] * len(weights)
    square = pltpu.VMEM((features, features), bf16)
    held = [] if total is None else [total if last else in_hbm(total)]
    at = len(tables) + len(known)
    outs = [pltpu.VMEM((views, length, features), f32)]
    if last:
        outs.append(jax.ShapeDtypeStruct((views, keys, features), bf16))
    return pl.pallas_call(
        functools.partial(attend_kernel, slots, len(sources), total is None, bool(last), keys),
        in_specs=[SMEM] * len(tables)
        + [VMEM, *weight_specs]
        + [VMEM] * len(last)
        + [VMEM if last else HBM] * len(held)
        + [ANY] * len(sources),
        out_specs=[VMEM] * len(outs),
        out_shape=outs,
        input_output_aliases={at: 0} if last else {},
        scratch_shapes=[
            pltpu.VMEM((2, length, features), bf16),
            pltpu.VMEM((length, 2 * features), bf16),
            pltpu.SMEM((len(slots),), jnp.int32),
            pltpu.SemaphoreType.DMA((2, len(slots[0][1]))),
            *(() if last else (square, square, pltpu.SemaphoreType.DMA((3,)))),
        ],
        compiler_params=pltpu.CompilerParams(vmem_limit_bytes=VMEM_LIMIT),
        cost_estimate=LARGE,
        name="attend",
    )(*tables, *known, *held, *sources)


def per_device(tokens, w_query, w_key, w_value, w_out, partners, counts, key_slot):
    views, length, features = tokens.shape
    degree = partners.shape[1]
    entries = views * degree
    row, column = lax.axis_index("row"), lax.axis_index("column")

    ids = partners.reshape(-1)
    peers = (ids // views) % (ROWS * COLS)
    codes = (peers // COLS - row) % ROWS * COLS + (peers % COLS - column) % COLS
    numbers = jnp.arange(entries, dtype=jnp.int32)
    live = (numbers % degree)[None, :] < jnp.repeat(counts, degree)[None, :]
    hit = (codes[None, :] == jnp.arange(ROWS * COLS, dtype=jnp.int32)[:, None]) & live
    slot_entry = jnp.max(jnp.where(hit, numbers[None, :], -1), axis=1)
    slot_place = jnp.sum(jnp.where(hit, (ids % views)[None, :], 0), axis=1)
    entry_table = jnp.concatenate([slot_entry, jnp.array([entries, entries + 1], jnp.int32)])
    place_table = jnp.concatenate([slot_place, jnp.zeros((2,), jnp.int32)])
    slot_key = key_slot[0]
    view_table = jnp.concatenate([numbers // degree, jnp.stack([slot_key, slot_key])])
    is_key = (jnp.arange(views, dtype=jnp.int32) == slot_key).astype(jnp.int32)
    divisor = 1.0 / (counts + 2 * is_key).astype(jnp.float32)
    key_share = jnp.sum(jnp.where(is_key == 1, divisor, 0.0))
    share_table = jnp.concatenate([jnp.repeat(divisor, degree), jnp.stack([key_share, key_share])])
    tables = (entry_table, place_table, view_table, share_table)

    tokens = jnp.pad(tokens, ((0, 0), (0, -length % 8), (0, 0)))
    chunks = range(len(CHUNKS))
    own = [tokens[:, low:high] for low, high in CHUNKS]
    down = [own] + [[None] * len(CHUNKS) for _ in range(4)]
    up = [own] + [[None] * len(CHUNKS) for _ in range(4)]

    def pass_on(s, c):
        below, above = down[s][c], up[s][c]
        if s == 3:
            below, above = below[: views // 2], above[views // 2 :]
        down[s + 1][c], up[s + 1][c] = shifted(below, "row", 1), shifted(above, "row", -1)

    for c in chunks:
        pass_on(0, c)
    asked = lax.all_gather(slot_place, "column", tiled=True)
    key_at, _ = lax.optimization_barrier((slot_key, slot_place))
    key_view = lax.dynamic_slice_in_dim(tokens, key_at, 1, axis=0)
    key_parts = [key_view[:, low:high] for low, high in CHUNKS]
    below = [shifted(x, "group", 1) for x in key_parts]
    above = [shifted(x, "group", -1) for x in key_parts]
    queries = project_queries(tokens, w_query)
    below, above, asked = lax.optimization_barrier((below, above, asked))
    queries = kept(queries)
    full = (0, views)
    halves = [(0, 0, views // 2), (1, views // 2, views)]

    def across(chosen):
        return [shifted(x, "column", -k) for k, x in zip(range(1, COLS), chosen)]

    picks = [(k, 0, k - 1, 0, [(0, 0, views)]) for k in range(1, COLS)]
    chosen = [pick(picks, asked, [x], 1) for x in own]
    arrived = [across(x) for x in chosen]
    done = queries, chosen[-1]
    waiting = [(c, x, 0, *full) for c, x in zip(KEY_CODES, (below, above))]
    waiting += [(k, [a[k - 1] for a in arrived], 0, *full) for k in range(1, COLS)]

    def run(waiting, total, last=()):
        sources, slots = [], []
        for code, arrays, lead, low, high in waiting:
            places = []
            for x in arrays:
                known = [i for i, y in enumerate(sources) if y is x]
                places.append(known[0] if known else len(sources))
                if not known:
                    sources.append(x)
            slots.append((code, tuple(places), lead, low, high))
        return attend(slots, tables, queries, w_key, w_value, length, total, sources, last)

    total = None
    for s in (1, 2, 3, 4):
        for c in chunks:
            (down[s][c], up[s][c]), done = lax.optimization_barrier(((down[s][c], up[s][c]), done))
            if s < 3:
                pass_on(s, c)
            if s < 4:
                picks = [
                    (k, r, k - 1, d, [(d, 0, views)])
                    for k in range(1, COLS)
                    for d, r in enumerate((ROWS - s, s))
                ]
            else:
                picks = [(k, 4, k - 1, 0, halves) for k in range(1, COLS)]
            chosen[c] = pick(picks, asked, [down[s][c], up[s][c]], 2 if s < 4 else 1)
            arrived[c] = across(chosen[c])
            done = chosen[c]
            if s == 3:
                (down[3][c], up[3][c]), done = lax.optimization_barrier(((down[3][c], up[3][c]), done))
                pass_on(3, c)
        if s < 4:
            waiting += [(h * COLS, x, None, *full) for h, x in ((ROWS - s, down[s]), (s, up[s]))]
        else:
            waiting += [(4 * COLS, (down[4], up[4])[h], None, low, high) for h, low, high in halves]
        queries, total, done = lax.optimization_barrier((queries, total, done))
        (total,) = run(waiting, total)
        done = done, total
        ahead = enumerate((ROWS - s, s) if s < 4 else (4,))
        waiting = [
            (r * COLS + k, [a[k - 1] for a in arrived], d, *full)
            for d, r in ahead
            for k in range(1, COLS)
        ]
    return run(waiting, total, last=(kept(tokens), kept(w_out)))[1]


def solution(mesh):
    finer = Mesh(mesh.devices.reshape(mesh.shape["group"], ROWS, COLS), ("group", "row", "column"))
    everywhere = ("group", "row", "column")
    placed = (
        P(everywhere, None, None),
        P(),
        P(),
        P(),
        P(),
        P(everywhere, None),
        P(everywhere),
        P(everywhere),
    )
    return jax.shard_map(
        per_device,
        mesh=finer,
        in_specs=placed,
        out_specs=P(everywhere, None, None),
        check_vma=False,
    )
```
